32 devices in a mesh: chan: 4 (over y, x), uv: 8 (over z, core).
Axes of the slice: x: 2, y: 2, z: 4, core: 2. Of those that a mesh axis runs over, the one named last changes fastest.
Arguments:
- visibilities: bfloat16 [16384, 2, 512], P('uv', None, 'chan'), may hold values from -3 to 3
- pair_patch_number: int32 [16384, 1], P('uv'), may hold values from 0 to 7; in each aligned block of 2048 rows (0 to 2047, 2048 to 4095, ...) at most 512 rows name the same one
- baseline_kernel_taps: bfloat16 [16384, 16], P('uv'), may hold values from 0.099609375 to 1
- kernel_start_cells: int32 [16384, 2], P('uv'), may hold values from 0 to 24
Outputs:
- spectra: float32 [8, 1024, 2, 512], P('uv', 'chan')
The draws below stay inside these ranges and needn't reach their ends.
Inputs may be any that keep to these rules, and one draw needn't show every extreme that they name: `pair_patch_number`: in each aligned block of 2048 baselines (the baselines of one index of uv) no subgrid is named more than 512 times, a bound that some block reaches.
All inputs are finite; a program needn't handle non-finite values.
Results may differ from the reference program's by a relative error of at most 0.004.
Values may be sent and summed in bfloat16 or wider, within the bound.
No kernel may reach another device: no remote copies, remote signals or barrier semaphores. Data moves between devices by JAX's collectives and lax.ppermute only.
A program may use at most 64 MiB of HBM per device.

```python
import math
import jax
import jax.numpy as jnp
import numpy as np
from jax import lax

SUBGRID_SIDE = 32
KERNEL_TAPS = 8
PAIRS_PER_SHARD = 2048
ANTENNA_PAIRS = 16384
PATCH_COUNT = 8
PAIRS_PER_PATCH = 512
CHANNEL_TOTAL = 512
N_UV = 8


def plant(array, stream_key, low, largest):
    extent = array.shape
    index_at = [jax.random.randint(jax.random.fold_in(stream_key, axis), (), 0, extent[axis]) for axis in range(len(extent))]
    array = array.at[tuple(index_at)].set(low)
    longest = extent.index(max(extent))
    index_at[longest] = (index_at[longest] + 1) % extent[longest]
    return array.at[tuple(index_at)].set(largest)


def block_levels(stream_key, extent, cuts, smallest, largest):
    factor_of, own = 1.0, jax.random.fold_in(stream_key, 6)
    for position, shards_of in cuts:
        draws = jnp.exp(jax.random.uniform(jax.random.fold_in(own, position), (shards_of,), jnp.float32, smallest / len(cuts), largest / len(cuts)))
        factor_of = factor_of * jnp.repeat(draws, extent[position] // shards_of).reshape([-1 if axis == position else 1 for axis in range(len(extent))])
    return factor_of


def shared_out(key, own, number, rows, count, top, reach, slope):
    order = jax.random.permutation(key, count)
    crowded, ordinary = load_shares(count, rows * top, reach, slope, True), load_shares(count, rows * top, reach, slope, False)
    places = jnp.arange(count)

    def named(lengths, offset_by):
        used = int((lengths > 0).sum())
        fixed = max(1, used // 4)
        passed = fixed + (places - fixed + offset_by * (used - fixed)) % max(1, count - fixed)
        return jnp.zeros((count,), jnp.int32).at[order[jnp.where(places < fixed, places, passed)]].set(jnp.asarray(lengths, jnp.int32))

    lengths = jnp.where(number % 4 == 0, named(crowded, number // 4), named(ordinary, number - number // 4 - 1))
    mixed = jax.random.permutation(jax.random.fold_in(own, 3), count)
    donor, receiver = mixed[0:count // 2 * 2:2], mixed[1:count // 2 * 2:2]
    margin = jnp.minimum(lengths[donor] - 1, reach - lengths[receiver]) // 2
    margin = jnp.where((donor == order[0]) | (receiver == order[0]) | (lengths[receiver] == 0), 0, jnp.maximum(margin, 0))
    passed = jax.random.randint(jax.random.fold_in(own, 4), (count // 2,), 0, 1 << 20) % (margin + 1)
    lengths = lengths.at[donor].add(-passed).at[receiver].add(passed)
    items = jnp.searchsorted(jnp.cumsum(lengths), jnp.arange(rows * top), side="right").astype(jnp.int32)
    listing = items.reshape(top, rows).T
    listing = listing[jax.random.permutation(jax.random.fold_in(own, 1), rows)]
    offset_by = jax.random.randint(jax.random.fold_in(own, 2), (rows, 1), 0, top)
    return jnp.take_along_axis(listing, (jnp.arange(top)[None, :] + offset_by) % top, axis=1)


def load_shares(number_of, total, reach, lean, full):
    portions = [(1 << 20) // math.isqrt(grade ** lean) + 1 for grade in range(1, number_of + 1)]
    largest = reach if full else min(reach, max(-(-total // number_of), total * portions[0] // sum(portions)))
    least = 1 if total - largest >= number_of - 1 else 0
    given, spare = [largest] + [least] * (number_of - 1), total - largest - least * (number_of - 1)
    while spare > 0:
        candidates = [i for i in range(1, number_of) if given[i] < largest] or [i for i in range(1, number_of) if given[i] < reach]
        whole, budget = sum([portions[i] for i in candidates]), spare
        for i in candidates:
            addition = min(reach - given[i], max(1, budget * portions[i] // whole), spare)
            given[i] = given[i] + addition
            spare = spare - addition
    return np.array(given)


def scatter_about(own_key, dims, width, most, split=(), held_as=jnp.bfloat16):
    result = jax.random.normal(own_key, dims, jnp.float32) * width
    if len(split) > 0:
        result = block_levels(own_key, dims, split, -0.22, 0.18) * result
    return jnp.clip(result, min=-most, max=most).astype(held_as)


def setup_inputs(seed: int = 0) -> dict:
    streams_of = jax.random.split(jax.random.key(seed), 5)
    visibilities = scatter_about(streams_of[0], (ANTENNA_PAIRS, 2, CHANNEL_TOTAL), 0.5, 3.0, ((0, 8), (2, 4)))
    pair_patch_number_keys = jax.random.split(jax.random.fold_in(streams_of[1], 1), ANTENNA_PAIRS // PAIRS_PER_SHARD)
    pair_patch_number_turns = jax.random.permutation(jax.random.fold_in(streams_of[1], 3), ANTENNA_PAIRS // PAIRS_PER_SHARD)
    pair_patch_number = jax.vmap(lambda own, number: shared_out(jax.random.fold_in(streams_of[1], 2), own, number, PAIRS_PER_SHARD, PATCH_COUNT, 1, PAIRS_PER_PATCH, 2))(pair_patch_number_keys, pair_patch_number_turns).reshape((ANTENNA_PAIRS, 1))
    baseline_kernel_taps = jnp.clip(0.099609375 + 0.9003906 * jax.random.uniform(streams_of[2], (ANTENNA_PAIRS, 2 * KERNEL_TAPS), jnp.float32) ** block_levels(streams_of[2], (ANTENNA_PAIRS, 2 * KERNEL_TAPS), ((0, 8),), -0.2, 0.2), 0.099609375, 1.0).astype(jnp.bfloat16)
    kernel_start_cells = plant(jax.random.randint(streams_of[3], (ANTENNA_PAIRS, 2), 0, SUBGRID_SIDE - KERNEL_TAPS + 1), jax.random.fold_in(streams_of[3], 1), 0, SUBGRID_SIDE - KERNEL_TAPS).astype(jnp.int32)
    return {"visibilities": visibilities, "pair_patch_number": pair_patch_number, "baseline_kernel_taps": baseline_kernel_taps, "kernel_start_cells": kernel_start_cells}


def kernel_rows(taps_float, offsets_float, cells_side):
    cell_index = jnp.arange(cells_side, dtype=jnp.float32)
    tap_index = jnp.arange(KERNEL_TAPS, dtype=jnp.float32)

    def one_axis(tap_values, opening_pixel):
        matches = (cell_index[None, None, :] == opening_pixel[:, None, None] + tap_index[None, :, None]).astype(jnp.float32)
        return lax.optimization_barrier(jnp.sum(tap_values[:, :, None] * matches, axis=1))
    return (one_axis(taps_float[:, :KERNEL_TAPS], offsets_float[:, 0]), one_axis(taps_float[:, KERNEL_TAPS:2 * KERNEL_TAPS], offsets_float[:, 1]))

def reference(visibilities, pair_patch_number, baseline_kernel_taps, kernel_start_cells):
    slot_count = N_UV * PAIRS_PER_PATCH
    flat_layout = visibilities.reshape(ANTENNA_PAIRS, 2 * CHANNEL_TOTAL)
    u_rows, v_rows = kernel_rows(baseline_kernel_taps.astype(jnp.float32), kernel_start_cells.astype(jnp.float32), SUBGRID_SIDE)
    subgrid_list = pair_patch_number[:, 0]

    def one_subgrid(subgrid_index):
        inside = subgrid_list == subgrid_index
        chosen = jnp.nonzero(inside, size=slot_count, fill_value=0)[0].astype(jnp.int32)
        live_mask = (jnp.arange(slot_count, dtype=jnp.int32) < jnp.sum(inside.astype(jnp.int32))).astype(jnp.float32)
        weights = v_rows[chosen][:, :, None] * u_rows[chosen][:, None, :] * live_mask[:, None, None]
        weights = weights.reshape(slot_count, SUBGRID_SIDE * SUBGRID_SIDE).astype(jnp.bfloat16)
        vis_rows = flat_layout[chosen]
        gridded = jnp.dot(weights.astype(jnp.float32).T, vis_rows.astype(jnp.float32), precision=lax.Precision.HIGHEST)
        gridded = lax.optimization_barrier(gridded.astype(jnp.bfloat16)).astype(jnp.float32).reshape(SUBGRID_SIDE * SUBGRID_SIDE, 2, CHANNEL_TOTAL)
        spectrum = jnp.fft.fft(gridded[:, 0] + 1j * gridded[:, 1], axis=-1) / math.sqrt(CHANNEL_TOTAL)
        return jnp.stack([jnp.real(spectrum), jnp.imag(spectrum)], axis=1).astype(jnp.float32)
    return lax.map(one_subgrid, jnp.arange(PATCH_COUNT, dtype=jnp.int32))
```

```python
import functools
import math

import jax
import jax.numpy as jnp
import numpy as np
from jax import lax
from jax.experimental import pallas as pl
from jax.experimental.pallas import tpu as pltpu
from jax.sharding import PartitionSpec as P

SUBGRID_SIDE = 32
KERNEL_TAPS = 8
CELLS = SUBGRID_SIDE * SUBGRID_SIDE
HALF = 256
META = 24
VMEM_LIMIT = 56 << 20


def sort_kernel(order_ref, patch_ref, meta_ref, vis_ref, out_ref, rank_ref):
    patch = patch_ref[...]
    groups, lanes = patch.shape
    uv_devices = 8

    @pl.when(pl.program_id(0) == 0)
    def _():
        members = jnp.concatenate(
            [(patch == s).astype(jnp.float32) for s in range(uv_devices)], axis=0
        ).astype(jnp.bfloat16)
        row = lax.broadcasted_iota(jnp.int32, (lanes, lanes), 0)
        col = lax.broadcasted_iota(jnp.int32, (lanes, lanes), 1)
        before = (row < col).astype(jnp.float32).astype(jnp.bfloat16)
        ahead = jnp.dot(members, before, preferred_element_type=jnp.float32)
        totals = jnp.dot(members, jnp.ones((lanes, lanes), jnp.bfloat16), preferred_element_type=jnp.float32)
        count = uv_devices * groups
        r = lax.broadcasted_iota(jnp.int32, (count, count), 0)
        c = lax.broadcasted_iota(jnp.int32, (count, count), 1)
        earlier = ((c < r) & (c // groups == r // groups)).astype(jnp.float32).astype(jnp.bfloat16)
        rank_all = ahead + jnp.dot(earlier, totals.astype(jnp.bfloat16), preferred_element_type=jnp.float32)
        rank = jnp.zeros((groups, lanes), jnp.float32)
        for s in range(uv_devices):
            rank = jnp.where(patch == s, rank_all[s * groups : (s + 1) * groups], rank)
        rank_ref[...] = rank

    s = order_ref[pl.program_id(0)]
    rank = rank_ref[...]
    slot = lax.broadcasted_iota(jnp.int32, (HALF, lanes), 0).astype(jnp.float32).astype(jnp.bfloat16)
    slot = slot.reshape(HALF // 16, 16, lanes)
    one = jnp.ones((), jnp.bfloat16)
    zero = jnp.zeros((), jnp.bfloat16)
    meta_parts = []
    for h in range(2):
        key = jnp.where(patch == s, rank - h * HALF, -1.0)
        key = jnp.where(key < HALF, key, -1.0)
        pieces = []
        for k in range(groups):
            k16 = jnp.broadcast_to(key[k : k + 1, :], (16, lanes)).astype(jnp.bfloat16)
            pieces.append(jnp.where(slot == k16[None], one, zero).reshape(HALF, lanes))
        select = jnp.concatenate(pieces, axis=1)
        rows = jnp.dot(select, vis_ref[...], preferred_element_type=jnp.float32)
        out_ref[0, h * HALF : (h + 1) * HALF, :] = rows.astype(jnp.bfloat16)
        meta = lax.dot_general(
            meta_ref[...], select, (((1,), (1,)), ((), ())), preferred_element_type=jnp.float32
        )
        meta_parts.append(meta[:META])
    out_ref[0, 2 * HALF :, :] = jnp.concatenate(meta_parts, axis=0).astype(jnp.bfloat16)


def sort_rows(order, patch, meta, vis):
    count = order.shape[0]
    return pl.pallas_call(
        sort_kernel,
        grid_spec=pltpu.PrefetchScalarGridSpec(
            num_scalar_prefetch=1,
            grid=(count,),
            in_specs=[
                pl.BlockSpec(patch.shape, lambda i, o: (0, 0)),
                pl.BlockSpec(meta.shape, lambda i, o: (0, 0)),
                pl.BlockSpec(vis.shape, lambda i, o: (0, 0)),
            ],
            out_specs=pl.BlockSpec((1, 2 * HALF + 2 * META, 256), lambda i, o: (i, 0, 0)),
            scratch_shapes=[pltpu.VMEM(patch.shape, jnp.float32)],
        ),
        out_shape=jax.ShapeDtypeStruct((count, 2 * HALF + 2 * META, 256), jnp.bfloat16),
        compiler_params=pltpu.CompilerParams(vmem_limit_bytes=VMEM_LIMIT),
        name="sort_rows",
    )(order, patch, meta, vis)


def spread(taps, start):
    cell = lax.broadcasted_iota(jnp.int32, (SUBGRID_SIDE, HALF), 0).astype(jnp.float32)
    offset = cell - start
    out = jnp.zeros((SUBGRID_SIDE, HALF), jnp.float32)
    for i in range(KERNEL_TAPS):
        out = jnp.where(offset == i, taps[i : i + 1, :], out)
    return out


def fill_weights(meta_block, weights_ref):
    meta = meta_block.astype(jnp.float32)
    for h in range(2):
        part = meta[h * META : (h + 1) * META]
        u = spread(part[:KERNEL_TAPS], part[16:17])
        v = spread(part[KERNEL_TAPS : 2 * KERNEL_TAPS], part[17:18])
        for y in range(SUBGRID_SIDE):
            weights_ref[y * SUBGRID_SIDE : (y + 1) * SUBGRID_SIDE, h * HALF : (h + 1) * HALF] = (
                v[y : y + 1, :] * u
            ).astype(jnp.bfloat16)


def grid_kernel(place_ref, rows_ref, out_ref, weights_ref, acc_ref):
    step = pl.program_id(0)

    @pl.when(step == 0)
    def _():
        acc_ref[...] = jnp.zeros_like(acc_ref)

    fill_weights(rows_ref[0, 2 * HALF :, :], weights_ref)
    acc_ref[...] += jnp.dot(
        weights_ref[...], rows_ref[0, : 2 * HALF, :], preferred_element_type=jnp.float32
    )

    @pl.when(step == pl.num_programs(0) - 1)
    def _():
        part = CELLS // 4
        for d in range(4):
            begin = pl.multiple_of((place_ref[0] ^ d) * part, part)
            out_ref[d] = acc_ref[pl.ds(begin, part), :].astype(jnp.bfloat16)


def grid_rows(place, rows):
    count = rows.shape[0]
    return pl.pallas_call(
        grid_kernel,
        grid_spec=pltpu.PrefetchScalarGridSpec(
            num_scalar_prefetch=1,
            grid=(count,),
            in_specs=[pl.BlockSpec((1,) + rows.shape[1:], lambda i, p: (i, 0, 0))],
            out_specs=pl.BlockSpec((4, CELLS // 4, 256), lambda i, p: (0, 0, 0)),
            scratch_shapes=[
                pltpu.VMEM((CELLS, 2 * HALF), jnp.bfloat16),
                pltpu.VMEM((CELLS, 256), jnp.float32),
            ],
        ),
        out_shape=jax.ShapeDtypeStruct((4, CELLS // 4, 256), jnp.bfloat16),
        compiler_params=pltpu.CompilerParams(vmem_limit_bytes=VMEM_LIMIT),
        name="grid_rows",
    )(place, rows)


def transform_matrix(length, width):
    n = np.arange(length)
    angle = (n[:, None] * n[None, :] % length) * (2.0 * np.pi / length)
    blocks = length // width
    cos = (np.cos(angle) / math.sqrt(length)).reshape(blocks, width, length)
    sin = (np.sin(angle) / math.sqrt(length)).reshape(blocks, width, length)
    whole = np.concatenate([cos, sin], axis=1)
    high = whole.astype(jnp.bfloat16)
    low = (whole - high.astype(np.float64)).astype(jnp.bfloat16)
    return high, low


def transform_kernel(place_ref, x0_ref, x1_ref, x2_ref, x3_ref, high_ref, low_ref, out_ref):
    real = imag = None
    for d, ref in enumerate((x0_ref, x1_ref, x2_ref, x3_ref)):
        block = place_ref[0] ^ d
        x = ref[...]
        width = x.shape[1] // 2
        turned = jnp.concatenate([x[:, width:], -x[:, :width]], axis=1)
        for matrix in (high_ref[block], low_ref[block]):
            a = jnp.dot(x, matrix, preferred_element_type=jnp.float32)
            b = jnp.dot(turned, matrix, preferred_element_type=jnp.float32)
            real = a if real is None else real + a
            imag = b if imag is None else imag + b
    out_ref[:, 0, :] = real
    out_ref[:, 1, :] = imag


def transform(place, pieces, high, low):
    cells = pieces[0].shape[0]
    length = high.shape[2]
    vmem = pl.BlockSpec(memory_space=pltpu.VMEM)
    return pl.pallas_call(
        transform_kernel,
        in_specs=[pl.BlockSpec(memory_space=pltpu.SMEM)] + [vmem] * 6,
        out_specs=vmem,
        out_shape=jax.ShapeDtypeStruct((cells, 2, length), jnp.float32),
        compiler_params=pltpu.CompilerParams(vmem_limit_bytes=VMEM_LIMIT),
        name="transform",
    )(place, *pieces, high, low)


def on_device_small(visibilities, pair_patch_number, baseline_kernel_taps, kernel_start_cells):
    rows_here, parts_count, channels = visibilities.shape
    vis = visibilities.reshape(rows_here, parts_count * channels)
    patch = pair_patch_number.reshape(rows_here // 128, 128)
    meta = jnp.concatenate(
        [
            baseline_kernel_taps.T,
            kernel_start_cells.astype(jnp.bfloat16).T,
            jnp.zeros((14, rows_here), jnp.bfloat16),
        ],
        axis=0,
    )
    chan = lax.axis_index("chan")
    place = chan.reshape(1).astype(jnp.int32)
    order = jnp.arange(8, dtype=jnp.int32)
    blocks = sort_rows(order, patch, meta, vis)
    got = lax.all_to_all(blocks, "uv", split_axis=0, concat_axis=0, tiled=True)
    gridded = grid_rows(place, got)
    pieces = [gridded[0]]
    for d in range(1, 4):
        pieces.append(lax.ppermute(gridded[d], "chan", [(c, c ^ d) for c in range(4)]))
    high, low = transform_matrix(4 * channels, channels)
    return transform(place, pieces, jnp.asarray(high), jnp.asarray(low))[None]


def kernel_rows(taps_float, offsets_float, cells_side):
    cell_index = jnp.arange(cells_side, dtype=jnp.float32)
    tap_index = jnp.arange(KERNEL_TAPS, dtype=jnp.float32)

    def one_axis(tap_values, opening_pixel):
        matches = (
            cell_index[None, None, :] == opening_pixel[:, None, None] + tap_index[None, :, None]
        ).astype(jnp.float32)
        return jnp.sum(tap_values[:, :, None] * matches, axis=1)

    return (
        one_axis(taps_float[:, :KERNEL_TAPS], offsets_float[:, 0]),
        one_axis(taps_float[:, KERNEL_TAPS : 2 * KERNEL_TAPS], offsets_float[:, 1]),
    )


def angle_table(row_count, col_count, period):
    row_ids = jnp.arange(row_count, dtype=jnp.int32)[:, None]
    col_ids = jnp.arange(col_count, dtype=jnp.int32)[None, :]
    angles = (row_ids * col_ids % period).astype(jnp.float32) * (2.0 * math.pi / period)
    return (jnp.cos(angles), jnp.sin(angles))


def delay_transform(pencil_data):
    leading, cell_count, parts_count, length = pencil_data.shape
    inner_len = 128
    outer_len = length // inner_len
    fine = lax.Precision.HIGH
    wide = jnp.float32
    values = pencil_data.reshape(leading * cell_count, parts_count, outer_len, inner_len)
    real_part = values[:, 0]
    imag_part = values[:, 1]
    cos_outer, sin_outer = angle_table(outer_len, outer_len, outer_len)
    first_real = jnp.einsum(
        "kn,mnj->mkj", cos_outer, real_part, precision=fine, preferred_element_type=wide
    ) + jnp.einsum("kn,mnj->mkj", sin_outer, imag_part, precision=fine, preferred_element_type=wide)
    first_imag = jnp.einsum(
        "kn,mnj->mkj", cos_outer, imag_part, precision=fine, preferred_element_type=wide
    ) - jnp.einsum("kn,mnj->mkj", sin_outer, real_part, precision=fine, preferred_element_type=wide)
    cos_twist, sin_twist = angle_table(outer_len, inner_len, length)
    twisted_real = first_real * cos_twist + first_imag * sin_twist
    twisted_imag = first_imag * cos_twist - first_real * sin_twist
    cos_inner, sin_inner = angle_table(inner_len, inner_len, inner_len)
    final_real = jnp.einsum("mkn,nq->mqk", twisted_real, cos_inner, precision=fine) + jnp.einsum(
        "mkn,nq->mqk", twisted_imag, sin_inner, precision=fine
    )
    final_imag = jnp.einsum("mkn,nq->mqk", twisted_imag, cos_inner, precision=fine) - jnp.einsum(
        "mkn,nq->mqk", twisted_real, sin_inner, precision=fine
    )
    scaling = 1.0 / math.sqrt(length)
    stacked = (
        jnp.stack([final_real.reshape(-1, length), final_imag.reshape(-1, length)], axis=1)
        * scaling
    )
    return stacked.reshape(leading, cell_count, parts_count, length)


def on_device_large(visibilities, pair_patch_number, baseline_kernel_taps, kernel_start_cells):
    rows_here, parts_count, frequency_bins = visibilities.shape
    uv_devices = lax.axis_size("uv")
    capacity = 2 * rows_here // uv_devices
    slot_count = uv_devices * capacity
    flat_layout = visibilities.reshape(rows_here, parts_count * frequency_bins)
    subgrid_list = pair_patch_number[:, 0]
    member = (subgrid_list[:, None] == jnp.arange(uv_devices, dtype=jnp.int32)[None, :]).astype(
        jnp.int32
    )
    preceding = jnp.sum((jnp.cumsum(member, axis=0) - member) * member, axis=1)
    target = subgrid_list * capacity + preceding
    vis_buffer = (
        jnp.zeros((slot_count, parts_count * frequency_bins), jnp.bfloat16)
        .at[target]
        .set(flat_layout)
    )
    vis_buffer = vis_buffer.reshape(uv_devices, capacity, parts_count * frequency_bins)
    u_rows, v_rows = kernel_rows(
        baseline_kernel_taps.astype(jnp.float32),
        kernel_start_cells.astype(jnp.float32),
        SUBGRID_SIDE,
    )
    payload = jnp.concatenate([u_rows, v_rows], axis=1).astype(jnp.bfloat16)
    payload_buffer = jnp.zeros((slot_count, 2 * SUBGRID_SIDE), jnp.bfloat16).at[target].set(payload)
    got_vis, got_payload = (
        lax.all_to_all(vis_buffer, "uv", split_axis=0, concat_axis=0, tiled=True),
        lax.all_to_all(
            payload_buffer.reshape(uv_devices, capacity, 2 * SUBGRID_SIDE),
            "uv",
            split_axis=0,
            concat_axis=0,
            tiled=True,
        ),
    )

    def kernels(payload_block):
        widened = payload_block.astype(jnp.float32)
        return (widened[:, :SUBGRID_SIDE], widened[:, SUBGRID_SIDE:])

    got_vis = got_vis.reshape(slot_count, parts_count * frequency_bins)
    got_payload = got_payload.reshape(slot_count, -1)
    stride = math.gcd(slot_count, 256)
    turn_count = slot_count // stride

    def accumulate(counter, accumulated):
        starting = counter * stride
        vis_block = lax.dynamic_slice_in_dim(got_vis, starting, stride, 0)
        payload_block = lax.dynamic_slice_in_dim(got_payload, starting, stride, 0)
        u_block, v_block = kernels(payload_block)
        weights = (
            (v_block[:, :, None] * u_block[:, None, :])
            .reshape(stride, SUBGRID_SIDE * SUBGRID_SIDE)
            .astype(jnp.bfloat16)
        )
        return accumulated + lax.dot_general(
            weights, vis_block, (((0,), (0,)), ((), ())), preferred_element_type=jnp.float32
        )

    gridded = lax.fori_loop(
        0,
        turn_count,
        accumulate,
        jnp.zeros((SUBGRID_SIDE * SUBGRID_SIDE, parts_count * frequency_bins), jnp.float32),
    )
    gridded = gridded.astype(jnp.bfloat16)
    chan_devices = lax.axis_size("chan")
    pieces = gridded.reshape(
        chan_devices, SUBGRID_SIDE * SUBGRID_SIDE // chan_devices, parts_count, frequency_bins
    )
    return delay_transform(lax.all_to_all(pieces, "chan", split_axis=0, concat_axis=3, tiled=True))


def solution(mesh):
    in_specs = (P("uv", None, "chan"), P("uv", None), P("uv", None), P("uv", None))
    out_specs = P("uv", "chan", None, None)
    small = mesh.shape["uv"] == 8 and mesh.shape["chan"] == 4
    return jax.shard_map(
        on_device_small if small else on_device_large,
        mesh=mesh,
        in_specs=in_specs,
        out_specs=out_specs,
        check_vma=False,
    )
```

```python
import functools
import math

import jax
import jax.numpy as jnp
import numpy as np
from jax import lax
from jax.experimental import pallas as pl
from jax.experimental.pallas import tpu as pltpu
from jax.sharding import PartitionSpec as P

SUBGRID_SIDE = 32
KERNEL_TAPS = 8
CELLS = SUBGRID_SIDE * SUBGRID_SIDE
HALF = 256
SLOTS = 2 * HALF
META = 32
VMEM_LIMIT = 24 << 20
VMEM_SPEC = pl.BlockSpec(memory_space=pltpu.VMEM)
SMEM_SPEC = pl.BlockSpec(memory_space=pltpu.SMEM)
PARAMS = pltpu.CompilerParams(vmem_limit_bytes=VMEM_LIMIT)


def on_chip(x):
    return pltpu.with_memory_space_constraint(x, pltpu.VMEM)


def tensor_dot(a, b, dims):
    return lax.dot_general(a, b, (dims, ((), ())), preferred_element_type=jnp.float32)


def place_rows(patch):
    groups, lanes = patch.shape
    members = jnp.concatenate([(patch == s).astype(jnp.float32) for s in range(8)], axis=0).astype(jnp.bfloat16)
    row = lax.broadcasted_iota(jnp.int32, (lanes, lanes), 0)
    col = lax.broadcasted_iota(jnp.int32, (lanes, lanes), 1)
    before = (row < col).astype(jnp.float32).astype(jnp.bfloat16)
    ahead = tensor_dot(members, before, ((1,), (0,)))
    totals = tensor_dot(members, jnp.ones((lanes, lanes), jnp.bfloat16), ((1,), (0,)))
    r = lax.broadcasted_iota(jnp.int32, (8 * groups, 8 * groups), 0)
    c = lax.broadcasted_iota(jnp.int32, (8 * groups, 8 * groups), 1)
    earlier = ((c < r) & (c // groups == r // groups)).astype(jnp.float32).astype(jnp.bfloat16)
    rank_all = ahead + tensor_dot(earlier, totals.astype(jnp.bfloat16), ((1,), (0,)))
    rank = jnp.zeros((groups, lanes), jnp.float32)
    for s in range(8):
        rank = jnp.where(patch == s, rank_all[s * groups : (s + 1) * groups], rank)
    return rank


def sort_into(target, patch, rank, columns_ref, out_ref):
    groups, lanes = patch.shape
    slot = lax.broadcasted_iota(jnp.int32, (HALF, lanes), 0).astype(jnp.float32).astype(jnp.bfloat16)
    slot = slot.reshape(HALF // 16, 16, lanes)
    one = jnp.ones((), jnp.bfloat16)
    zero = jnp.zeros((), jnp.bfloat16)

    def selection(h):
        key = jnp.where(patch == target, rank - h * HALF, -1.0)
        key = jnp.where(key < HALF, key, -1.0)
        pieces = []
        for k in range(groups):
            k16 = jnp.broadcast_to(key[k : k + 1, :], (16, lanes)).astype(jnp.bfloat16)
            pieces.append(jnp.where(slot == k16[None], one, zero).reshape(HALF, lanes))
        return jnp.concatenate(pieces, axis=1)

    select = jnp.concatenate([selection(0), selection(1)], axis=0)
    out_ref[...] = tensor_dot(columns_ref[...], select, ((1,), (1,))).astype(jnp.bfloat16)


def target_z(z, which):
    if which == "far":
        return jnp.where(z < 2, 3, 0)
    if which == "near":
        return jnp.where(z < 2, 2, 1)
    return z ^ 1 if which == "beside" else z


def sort_far(uv, patch, taps, starts, vis):
    rows, parts, channels = vis.shape
    width = parts * channels

    def kernel(
        uv_ref, patch_hbm, taps_hbm, starts_hbm, vis_hbm, far0_ref, far1_ref, columns_ref, rank_ref,
        patch_ref, taps_ref, starts_ref, vis_ref, sems,
    ):
        copies = [
            pltpu.make_async_copy(patch_hbm, patch_ref, sems.at[0]),
            pltpu.make_async_copy(vis_hbm, vis_ref, sems.at[1]),
            pltpu.make_async_copy(taps_hbm, taps_ref, sems.at[2]),
            pltpu.make_async_copy(starts_hbm, starts_ref, sems.at[3]),
        ]
        for copy in copies:
            copy.start()
        copies[0].wait()
        patch = patch_ref[...]
        rank_ref[...] = place_rows(patch)
        copies[2].wait()
        copies[3].wait()
        patch_f = patch.astype(jnp.float32)
        columns_ref[width:, :] = jnp.concatenate(
            [
                taps_ref[...].astype(jnp.float32),
                starts_ref[...].astype(jnp.float32),
                jnp.concatenate([patch_f[k : k + 1, :] for k in range(patch.shape[0])], axis=1),
                jnp.zeros((META - 2 * KERNEL_TAPS - 3, rows), jnp.float32),
            ],
            axis=0,
        ).astype(jnp.bfloat16)
        copies[1].wait()
        columns_ref[:width, :] = vis_ref[...].reshape(rows, width).T
        target = 2 * target_z(uv_ref[0] // 2, "far") + uv_ref[0] % 2
        sort_into(target, patch, rank_ref[...], columns_ref, far0_ref)
        sort_into(target ^ 1, patch, rank_ref[...], columns_ref, far1_ref)

    in_hbm = [pltpu.with_memory_space_constraint(x, pltpu.HBM) for x in (patch, taps, starts, vis)]
    block = pltpu.VMEM((width + META, SLOTS), jnp.bfloat16)
    return pl.pallas_call(
        kernel,
        in_specs=[SMEM_SPEC] + [pl.BlockSpec(memory_space=pl.ANY)] * 4,
        out_specs=[VMEM_SPEC] * 4,
        out_shape=[
            block,
            block,
            pltpu.VMEM((width + META, rows), jnp.bfloat16),
            pltpu.VMEM(patch.shape, jnp.float32),
        ],
        scratch_shapes=[pltpu.VMEM(x.shape, x.dtype) for x in (patch, taps, starts, vis)]
        + [pltpu.SemaphoreType.DMA((4,))],
        compiler_params=PARAMS,
        name="sort_far",
    )(uv, *in_hbm)


def patch_of(columns_ref, lanes):
    at = columns_ref.shape[0] - META + 2 * KERNEL_TAPS
    row = columns_ref[at : at + 16, :].astype(jnp.float32)[2:3, :]
    pieces = [row[:, k * lanes : (k + 1) * lanes] for k in range(row.shape[1] // lanes)]
    return jnp.concatenate(pieces, axis=0).astype(jnp.int32)


def sort_near(uv, rank, columns, columns2):
    def kernel(uv_ref, rank_ref, columns_ref, columns2_ref, near_ref, far_ref, rank2_ref):
        z, core = uv_ref[0] // 2, uv_ref[0] % 2
        target = 2 * target_z(z, "near") + core
        patch2 = patch_of(columns2_ref, rank_ref.shape[1])
        rank2_ref[...] = place_rows(patch2)
        sort_into(target, patch_of(columns_ref, rank_ref.shape[1]), rank_ref[...], columns_ref, near_ref.at[0])
        sort_into(target, patch2, rank2_ref[...], columns2_ref, near_ref.at[1])
        sort_into(2 * target_z(z, "far") + core, patch2, rank2_ref[...], columns2_ref, far_ref)

    return pl.pallas_call(
        kernel,
        in_specs=[SMEM_SPEC] + [VMEM_SPEC] * 3,
        out_specs=[VMEM_SPEC] * 3,
        out_shape=[
            pltpu.VMEM((2, columns.shape[0], SLOTS), jnp.bfloat16),
            pltpu.VMEM((columns.shape[0], SLOTS), jnp.bfloat16),
            pltpu.VMEM(rank.shape, jnp.float32),
        ],
        compiler_params=PARAMS,
        name="sort_near",
    )(uv, on_chip(rank), on_chip(columns), on_chip(columns2))


def sort_rest(uv, rank, rank2, columns, columns2):
    def kernel(uv_ref, rank_ref, rank2_ref, columns_ref, columns2_ref, beside_ref, own_ref):
        z, core = uv_ref[0] // 2, uv_ref[0] % 2
        patch = patch_of(columns_ref, rank_ref.shape[1])
        patch2 = patch_of(columns2_ref, rank_ref.shape[1])
        for which, ref in (("beside", beside_ref), ("own", own_ref)):
            target = 2 * target_z(z, which) + core
            sort_into(target, patch, rank_ref[...], columns_ref, ref.at[0])
            sort_into(target, patch2, rank2_ref[...], columns2_ref, ref.at[1])

    return pl.pallas_call(
        kernel,
        in_specs=[SMEM_SPEC] + [VMEM_SPEC] * 4,
        out_specs=[VMEM_SPEC] * 2,
        out_shape=[pltpu.VMEM((2, columns.shape[0], SLOTS), jnp.bfloat16)] * 2,
        compiler_params=PARAMS,
        name="sort_rest",
    )(uv, on_chip(rank), on_chip(rank2), on_chip(columns), on_chip(columns2))


def spread(taps, start):
    cell = lax.broadcasted_iota(jnp.int32, (SUBGRID_SIDE, SLOTS), 0).astype(jnp.float32)
    offset = cell - start
    out = jnp.zeros((SUBGRID_SIDE, SLOTS), jnp.float32)
    for i in range(KERNEL_TAPS):
        out = jnp.where(offset == i, taps[i : i + 1, :], out)
    return out


def grid_block(block_ref, weights_ref):
    width = block_ref.shape[0] - META
    meta = block_ref[width:, :].astype(jnp.float32)
    u = spread(meta[:KERNEL_TAPS], meta[2 * KERNEL_TAPS : 2 * KERNEL_TAPS + 1])
    v = spread(meta[KERNEL_TAPS : 2 * KERNEL_TAPS], meta[2 * KERNEL_TAPS + 1 : 2 * KERNEL_TAPS + 2])
    for y in range(SUBGRID_SIDE):
        weights_ref[y * SUBGRID_SIDE : (y + 1) * SUBGRID_SIDE, :] = (v[y : y + 1, :] * u).astype(jnp.bfloat16)
    return tensor_dot(weights_ref[...], block_ref[:width, :], ((1,), (1,)))


WEIGHTS = [pltpu.VMEM((CELLS, SLOTS), jnp.bfloat16)]


def grid_total(block_refs, weights_ref, total=None):
    for ref in block_refs:
        for block_ref in [ref.at[0], ref.at[1]] if len(ref.shape) == 3 else [ref]:
            term = grid_block(block_ref, weights_ref)
            total = term if total is None else total + term
    return total


def grid_rows(blocks, dtype, before=None):
    count = len(blocks)
    operands = [on_chip(x) for x in blocks]
    height = operands[0].shape[-2]
    if before is not None:
        operands.append(on_chip(before))

    def kernel(*refs):
        total = None if before is None else refs[count][...]
        refs[-2][...] = grid_total(refs[:count], refs[-1], total).astype(dtype)

    return pl.pallas_call(
        kernel,
        in_specs=[VMEM_SPEC] * len(operands),
        out_specs=VMEM_SPEC,
        out_shape=pltpu.VMEM((CELLS, height - META), dtype),
        scratch_shapes=WEIGHTS,
        compiler_params=PARAMS,
        name="grid_rows",
    )(*operands)


def finish(place, blocks, near, far):
    part = CELLS // 4
    count = len(blocks)

    def kernel(place_ref, *refs):
        near_ref, far_ref = refs[count], refs[count + 1]
        piece_refs, total_ref, weights_ref = refs[count + 2 : count + 6], refs[-2], refs[-1]
        total = near_ref[...] + far_ref[...].astype(jnp.float32)
        total_ref[...] = grid_total(refs[:count], weights_ref, total)
        for d, piece_ref in enumerate(piece_refs):
            cells = pl.ds(pl.multiple_of((place_ref[0] ^ d) * part, part), part)
            piece_ref[...] = total_ref[cells, :].astype(jnp.bfloat16)

    piece = pltpu.VMEM((part, near.shape[1]), jnp.bfloat16)
    return pl.pallas_call(
        kernel,
        in_specs=[SMEM_SPEC] + [VMEM_SPEC] * (count + 2),
        out_specs=[VMEM_SPEC] * 4,
        out_shape=[piece] * 4,
        scratch_shapes=[pltpu.VMEM(near.shape, jnp.float32)] + WEIGHTS,
        compiler_params=PARAMS,
        name="finish",
    )(place, *[on_chip(x) for x in blocks], on_chip(near), on_chip(far))


def transform_matrix(length, width):
    n = np.arange(length)
    angle = (n[:, None] * n[None, :] % length) * (2.0 * np.pi / length)
    blocks = length // width
    cos = (np.cos(angle) / math.sqrt(length)).reshape(blocks, width, length)
    sin = (np.sin(angle) / math.sqrt(length)).reshape(blocks, width, length)
    whole = np.concatenate([cos, sin], axis=1)
    high = whole.astype(jnp.bfloat16)
    low = (whole - high.astype(np.float64)).astype(jnp.bfloat16)
    return high, low


def transform_kernel(place_ref, x0_ref, x1_ref, x2_ref, x3_ref, high_ref, low_ref, out_ref):
    real = imag = None
    for d, ref in enumerate((x0_ref, x1_ref, x2_ref, x3_ref)):
        block = place_ref[0] ^ d
        x = ref[...]
        width = x.shape[1] // 2
        turned = jnp.concatenate([x[:, width:], -x[:, :width]], axis=1)
        for matrix in (high_ref[block], low_ref[block]):
            a = jnp.dot(x, matrix, preferred_element_type=jnp.float32)
            b = jnp.dot(turned, matrix, preferred_element_type=jnp.float32)
            real = a if real is None else real + a
            imag = b if imag is None else imag + b
    out_ref[:, 0, :] = real
    out_ref[:, 1, :] = imag


def transform(place, pieces, high, low):
    return pl.pallas_call(
        transform_kernel,
        in_specs=[SMEM_SPEC] + [VMEM_SPEC] * 6,
        out_specs=VMEM_SPEC,
        out_shape=jax.ShapeDtypeStruct((pieces[0].shape[0], 2, high.shape[2]), jnp.float32),
        compiler_params=PARAMS,
        name="transform",
    )(place, *[on_chip(x) for x in pieces], on_chip(high), on_chip(low))


def on_device_small(visibilities, pair_patch_number, baseline_kernel_taps, kernel_start_cells):
    rows_here, parts_count, channels = visibilities.shape
    patch = pair_patch_number.reshape(rows_here // 128, 128)
    place = lax.axis_index("chan").astype(jnp.int32).reshape(1)
    uv = lax.axis_index("uv").astype(jnp.int32).reshape(1)

    def send(block, pairs, j=0):
        return lax.ppermute(block, "uv", [(2 * a + c, 2 * b + (c ^ j)) for a, b in pairs for c in range(2)])

    def swap(block):
        return lax.ppermute(block, "uv", [(u, u ^ 1) for u in range(8)])

    far0, far1, columns, rank = sort_far(uv, patch, baseline_kernel_taps.T, kernel_start_cells.T, visibilities)
    far_in = [send(far0, [(0, 1), (3, 2)]), send(far1, [(0, 1), (3, 2)], 1)]
    columns2 = swap(columns)
    near, far2, rank2 = sort_near(uv, rank, columns, columns2)
    near_in = send(near, [(1, 2), (2, 1)])
    near_in2 = send(near, [(0, 2), (3, 1)])

    merged = grid_rows([far0, far2, *far_in], jnp.bfloat16)
    merged_in = send(merged, [(1, 3), (2, 0)])
    rank2, _ = lax.optimization_barrier((rank2, merged))
    beside, own = sort_rest(uv, rank, rank2, columns, columns2)
    beside_in = send(beside, [(0, 1), (1, 0), (2, 3), (3, 2)])
    near_in, own = lax.optimization_barrier((near_in, own))
    grid = grid_rows([own, near_in], jnp.float32)
    near_in2, grid = lax.optimization_barrier((near_in2, grid))
    grid = grid_rows([near_in2], jnp.float32, grid)
    beside_in, merged_in, grid = lax.optimization_barrier((beside_in, merged_in, grid))
    pieces = finish(place, [beside_in], grid, merged_in)
    got = [pieces[0]]
    for d in range(1, 4):
        got.append(lax.ppermute(pieces[d], "chan", [(c, c ^ d) for c in range(4)]))
    high, low = transform_matrix(4 * channels, channels)
    return transform(place, got, jnp.asarray(high), jnp.asarray(low))[None]


def kernel_rows(taps_float, offsets_float, cells_side):
    cell_index = jnp.arange(cells_side, dtype=jnp.float32)
    tap_index = jnp.arange(KERNEL_TAPS, dtype=jnp.float32)

    def one_axis(tap_values, opening_pixel):
        matches = (
            cell_index[None, None, :] == opening_pixel[:, None, None] + tap_index[None, :, None]
        ).astype(jnp.float32)
        return jnp.sum(tap_values[:, :, None] * matches, axis=1)

    return (
        one_axis(taps_float[:, :KERNEL_TAPS], offsets_float[:, 0]),
        one_axis(taps_float[:, KERNEL_TAPS : 2 * KERNEL_TAPS], offsets_float[:, 1]),
    )


def angle_table(row_count, col_count, period):
    row_ids = jnp.arange(row_count, dtype=jnp.int32)[:, None]
    col_ids = jnp.arange(col_count, dtype=jnp.int32)[None, :]
    angles = (row_ids * col_ids % period).astype(jnp.float32) * (2.0 * math.pi / period)
    return (jnp.cos(angles), jnp.sin(angles))


def delay_transform(pencil_data):
    leading, cell_count, parts_count, length = pencil_data.shape
    inner_len = 128
    outer_len = length // inner_len
    fine = lax.Precision.HIGH
    wide = jnp.float32
    values = pencil_data.reshape(leading * cell_count, parts_count, outer_len, inner_len)
    real_part = values[:, 0]
    imag_part = values[:, 1]
    cos_outer, sin_outer = angle_table(outer_len, outer_len, outer_len)
    first_real = jnp.einsum(
        "kn,mnj->mkj", cos_outer, real_part, precision=fine, preferred_element_type=wide
    ) + jnp.einsum("kn,mnj->mkj", sin_outer, imag_part, precision=fine, preferred_element_type=wide)
    first_imag = jnp.einsum(
        "kn,mnj->mkj", cos_outer, imag_part, precision=fine, preferred_element_type=wide
    ) - jnp.einsum("kn,mnj->mkj", sin_outer, real_part, precision=fine, preferred_element_type=wide)
    cos_twist, sin_twist = angle_table(outer_len, inner_len, length)
    twisted_real = first_real * cos_twist + first_imag * sin_twist
    twisted_imag = first_imag * cos_twist - first_real * sin_twist
    cos_inner, sin_inner = angle_table(inner_len, inner_len, inner_len)
    final_real = jnp.einsum("mkn,nq->mqk", twisted_real, cos_inner, precision=fine) + jnp.einsum(
        "mkn,nq->mqk", twisted_imag, sin_inner, precision=fine
    )
    final_imag = jnp.einsum("mkn,nq->mqk", twisted_imag, cos_inner, precision=fine) - jnp.einsum(
        "mkn,nq->mqk", twisted_real, sin_inner, precision=fine
    )
    scaling = 1.0 / math.sqrt(length)
    stacked = (
        jnp.stack([final_real.reshape(-1, length), final_imag.reshape(-1, length)], axis=1)
        * scaling
    )
    return stacked.reshape(leading, cell_count, parts_count, length)


def on_device_large(visibilities, pair_patch_number, baseline_kernel_taps, kernel_start_cells):
    rows_here, parts_count, frequency_bins = visibilities.shape
    uv_devices = lax.axis_size("uv")
    capacity = 2 * rows_here // uv_devices
    slot_count = uv_devices * capacity
    flat_layout = visibilities.reshape(rows_here, parts_count * frequency_bins)
    subgrid_list = pair_patch_number[:, 0]
    member = (subgrid_list[:, None] == jnp.arange(uv_devices, dtype=jnp.int32)[None, :]).astype(
        jnp.int32
    )
    preceding = jnp.sum((jnp.cumsum(member, axis=0) - member) * member, axis=1)
    target = subgrid_list * capacity + preceding
    vis_buffer = (
        jnp.zeros((slot_count, parts_count * frequency_bins), jnp.bfloat16)
        .at[target]
        .set(flat_layout)
    )
    vis_buffer = vis_buffer.reshape(uv_devices, capacity, parts_count * frequency_bins)
    u_rows, v_rows = kernel_rows(
        baseline_kernel_taps.astype(jnp.float32),
        kernel_start_cells.astype(jnp.float32),
        SUBGRID_SIDE,
    )
    payload = jnp.concatenate([u_rows, v_rows], axis=1).astype(jnp.bfloat16)
    payload_buffer = jnp.zeros((slot_count, 2 * SUBGRID_SIDE), jnp.bfloat16).at[target].set(payload)
    got_vis, got_payload = (
        lax.all_to_all(vis_buffer, "uv", split_axis=0, concat_axis=0, tiled=True),
        lax.all_to_all(
            payload_buffer.reshape(uv_devices, capacity, 2 * SUBGRID_SIDE),
            "uv",
            split_axis=0,
            concat_axis=0,
            tiled=True,
        ),
    )

    def kernels(payload_block):
        widened = payload_block.astype(jnp.float32)
        return (widened[:, :SUBGRID_SIDE], widened[:, SUBGRID_SIDE:])

    got_vis = got_vis.reshape(slot_count, parts_count * frequency_bins)
    got_payload = got_payload.reshape(slot_count, -1)
    stride = math.gcd(slot_count, 256)
    turn_count = slot_count // stride

    def accumulate(counter, accumulated):
        starting = counter * stride
        vis_block = lax.dynamic_slice_in_dim(got_vis, starting, stride, 0)
        payload_block = lax.dynamic_slice_in_dim(got_payload, starting, stride, 0)
        u_block, v_block = kernels(payload_block)
        weights = (
            (v_block[:, :, None] * u_block[:, None, :])
            .reshape(stride, SUBGRID_SIDE * SUBGRID_SIDE)
            .astype(jnp.bfloat16)
        )
        return accumulated + lax.dot_general(
            weights, vis_block, (((0,), (0,)), ((), ())), preferred_element_type=jnp.float32
        )

    gridded = lax.fori_loop(
        0,
        turn_count,
        accumulate,
        jnp.zeros((SUBGRID_SIDE * SUBGRID_SIDE, parts_count * frequency_bins), jnp.float32),
    )
    gridded = gridded.astype(jnp.bfloat16)
    chan_devices = lax.axis_size("chan")
    pieces = gridded.reshape(
        chan_devices, SUBGRID_SIDE * SUBGRID_SIDE // chan_devices, parts_count, frequency_bins
    )
    return delay_transform(lax.all_to_all(pieces, "chan", split_axis=0, concat_axis=3, tiled=True))


def solution(mesh):
    in_specs = (P("uv", None, "chan"), P("uv", None), P("uv", None), P("uv", None))
    out_specs = P("uv", "chan", None, None)
    small = mesh.shape["uv"] == 8 and mesh.shape["chan"] == 4
    return jax.shard_map(
        on_device_small if small else on_device_large,
        mesh=mesh,
        in_specs=in_specs,
        out_specs=out_specs,
        check_vma=False,
    )
```

```python
import functools
import math

import jax
import jax.numpy as jnp
import numpy as np
from jax import lax
from jax.experimental import pallas as pl
from jax.experimental.pallas import tpu as pltpu
from jax.sharding import PartitionSpec as P

SUBGRID_SIDE = 32
KERNEL_TAPS = 8
CELLS = SUBGRID_SIDE * SUBGRID_SIDE
HALF = 256
SLOTS = 2 * HALF
META = 32
VMEM_LIMIT = 24 << 20
VMEM_SPEC = pl.BlockSpec(memory_space=pltpu.VMEM)
SMEM_SPEC = pl.BlockSpec(memory_space=pltpu.SMEM)
PARAMS = pltpu.CompilerParams(vmem_limit_bytes=VMEM_LIMIT)


def on_chip(x):
    return pltpu.with_memory_space_constraint(x, pltpu.VMEM)


def tensor_dot(a, b, dims):
    return lax.dot_general(a, b, (dims, ((), ())), preferred_element_type=jnp.float32)


def place_rows(patch):
    groups, lanes = patch.shape
    members = jnp.concatenate([(patch == s).astype(jnp.float32) for s in range(8)], axis=0).astype(jnp.bfloat16)
    row = lax.broadcasted_iota(jnp.int32, (lanes, lanes), 0)
    col = lax.broadcasted_iota(jnp.int32, (lanes, lanes), 1)
    before = (row < col).astype(jnp.float32).astype(jnp.bfloat16)
    ahead = tensor_dot(members, before, ((1,), (0,)))
    totals = tensor_dot(members, jnp.ones((lanes, lanes), jnp.bfloat16), ((1,), (0,)))
    r = lax.broadcasted_iota(jnp.int32, (8 * groups, 8 * groups), 0)
    c = lax.broadcasted_iota(jnp.int32, (8 * groups, 8 * groups), 1)
    earlier = ((c < r) & (c // groups == r // groups)).astype(jnp.float32).astype(jnp.bfloat16)
    rank_all = ahead + tensor_dot(earlier, totals.astype(jnp.bfloat16), ((1,), (0,)))
    rank = jnp.zeros((groups, lanes), jnp.float32)
    for s in range(8):
        rank = jnp.where(patch == s, rank_all[s * groups : (s + 1) * groups], rank)
    return rank


def sort_into(target, patch, rank, columns_ref, out_ref):
    groups, lanes = patch.shape
    slot = lax.broadcasted_iota(jnp.int32, (HALF, lanes), 0).astype(jnp.float32).astype(jnp.bfloat16)
    slot = slot.reshape(HALF // 16, 16, lanes)
    one = jnp.ones((), jnp.bfloat16)
    zero = jnp.zeros((), jnp.bfloat16)

    def selection(h):
        key = jnp.where(patch == target, rank - h * HALF, -1.0)
        key = jnp.where(key < HALF, key, -1.0)
        pieces = []
        for k in range(groups):
            k16 = jnp.broadcast_to(key[k : k + 1, :], (16, lanes)).astype(jnp.bfloat16)
            pieces.append(jnp.where(slot == k16[None], one, zero).reshape(HALF, lanes))
        return jnp.concatenate(pieces, axis=1)

    select = jnp.concatenate([selection(0), selection(1)], axis=0)
    out_ref[...] = tensor_dot(columns_ref[...], select, ((1,), (1,))).astype(jnp.bfloat16)


def sort_first(uv, patch, taps, starts, vis):
    rows, parts, channels = vis.shape
    width = parts * channels

    def kernel(
        uv_ref, patch_hbm, taps_hbm, starts_hbm, vis_hbm, first0_ref, first1_ref, first_ref, columns_ref, rank_ref,
        patch_ref, taps_ref, starts_ref, vis_ref, sems,
    ):
        copies = [
            pltpu.make_async_copy(patch_hbm, patch_ref, sems.at[0]),
            pltpu.make_async_copy(vis_hbm, vis_ref, sems.at[1]),
            pltpu.make_async_copy(taps_hbm, taps_ref, sems.at[2]),
            pltpu.make_async_copy(starts_hbm, starts_ref, sems.at[3]),
        ]
        for copy in copies:
            copy.start()
        copies[0].wait()
        patch = patch_ref[...]
        rank_ref[...] = place_rows(patch)
        copies[2].wait()
        copies[3].wait()
        patch_f = patch.astype(jnp.float32)
        columns_ref[width:, :] = jnp.concatenate(
            [
                taps_ref[...].astype(jnp.float32),
                starts_ref[...].astype(jnp.float32),
                jnp.concatenate([patch_f[k : k + 1, :] for k in range(patch.shape[0])], axis=1),
                jnp.zeros((META - 2 * KERNEL_TAPS - 3, rows), jnp.float32),
            ],
            axis=0,
        ).astype(jnp.bfloat16)
        copies[1].wait()
        columns_ref[:width, :] = vis_ref[...].reshape(rows, width).T
        target = 2 * (3 - uv_ref[0] // 2) + uv_ref[0] % 2
        for j, ref in enumerate((first0_ref, first1_ref)):
            sort_into(target ^ j, patch, rank_ref[...], columns_ref, ref)
            first_ref[j] = ref[...]

    in_hbm = [pltpu.with_memory_space_constraint(x, pltpu.HBM) for x in (patch, taps, starts, vis)]
    return pl.pallas_call(
        kernel,
        in_specs=[SMEM_SPEC] + [pl.BlockSpec(memory_space=pl.ANY)] * 4,
        out_specs=[VMEM_SPEC] * 5,
        out_shape=[
            pltpu.VMEM((width + META, SLOTS), jnp.bfloat16),
            pltpu.VMEM((width + META, SLOTS), jnp.bfloat16),
            pltpu.VMEM((2, width + META, SLOTS), jnp.bfloat16),
            pltpu.VMEM((width + META, rows), jnp.bfloat16),
            pltpu.VMEM(patch.shape, jnp.float32),
        ],
        scratch_shapes=[pltpu.VMEM(x.shape, x.dtype) for x in (patch, taps, starts, vis)]
        + [pltpu.SemaphoreType.DMA((4,))],
        compiler_params=PARAMS,
        name="sort_first",
    )(uv, *in_hbm)


def patch_of(columns_ref, lanes):
    at = columns_ref.shape[0] - META + 2 * KERNEL_TAPS
    row = columns_ref[at : at + 16, :].astype(jnp.float32)[2:3, :]
    pieces = [row[:, k * lanes : (k + 1) * lanes] for k in range(row.shape[1] // lanes)]
    return jnp.concatenate(pieces, axis=0).astype(jnp.int32)


def at_ends(z, end, middle):
    return jnp.where((z == 0) | (z == 3), end, middle)


def sort_second(uv, rank, columns, columns2):
    def kernel(uv_ref, rank_ref, columns_ref, columns2_ref, second_ref, rank2_ref):
        z, core = uv_ref[0] // 2, uv_ref[0] % 2
        target = 2 * at_ends(z, (3 - z) ^ 1, z ^ 1) + core
        patch2 = patch_of(columns2_ref, rank_ref.shape[1])
        rank2_ref[...] = place_rows(patch2)
        sort_into(target, patch_of(columns_ref, rank_ref.shape[1]), rank_ref[...], columns_ref, second_ref.at[0])
        sort_into(target, patch2, rank2_ref[...], columns2_ref, second_ref.at[1])

    return pl.pallas_call(
        kernel,
        in_specs=[SMEM_SPEC] + [VMEM_SPEC] * 3,
        out_specs=[VMEM_SPEC] * 2,
        out_shape=[
            pltpu.VMEM((2, columns.shape[0], SLOTS), jnp.bfloat16),
            pltpu.VMEM(rank.shape, jnp.float32),
        ],
        compiler_params=PARAMS,
        name="sort_second",
    )(uv, on_chip(rank), on_chip(columns), on_chip(columns2))


def sort_rest(uv, rank, rank2, columns, columns2):
    def kernel(uv_ref, rank_ref, rank2_ref, columns_ref, columns2_ref, third_ref, own_ref):
        z, core = uv_ref[0] // 2, uv_ref[0] % 2
        patch = patch_of(columns_ref, rank_ref.shape[1])
        patch2 = patch_of(columns2_ref, rank_ref.shape[1])
        third = 2 * at_ends(z, z ^ 1, (3 - z) ^ 1) + core
        for target, ref in ((third, third_ref), (uv_ref[0], own_ref)):
            sort_into(target, patch, rank_ref[...], columns_ref, ref.at[0])
            sort_into(target, patch2, rank2_ref[...], columns2_ref, ref.at[1])

    return pl.pallas_call(
        kernel,
        in_specs=[SMEM_SPEC] + [VMEM_SPEC] * 4,
        out_specs=[VMEM_SPEC] * 2,
        out_shape=[pltpu.VMEM((2, columns.shape[0], SLOTS), jnp.bfloat16)] * 2,
        compiler_params=PARAMS,
        name="sort_rest",
    )(uv, on_chip(rank), on_chip(rank2), on_chip(columns), on_chip(columns2))


def spread(taps, start):
    cell = lax.broadcasted_iota(jnp.int32, (SUBGRID_SIDE, SLOTS), 0).astype(jnp.float32)
    offset = cell - start
    out = jnp.zeros((SUBGRID_SIDE, SLOTS), jnp.float32)
    for i in range(KERNEL_TAPS):
        out = jnp.where(offset == i, taps[i : i + 1, :], out)
    return out


def fill_weights(meta, weights_ref):
    meta = meta.astype(jnp.float32)
    u = spread(meta[:KERNEL_TAPS], meta[2 * KERNEL_TAPS : 2 * KERNEL_TAPS + 1])
    v = spread(meta[KERNEL_TAPS : 2 * KERNEL_TAPS], meta[2 * KERNEL_TAPS + 1 : 2 * KERNEL_TAPS + 2])
    for y in range(SUBGRID_SIDE):
        weights_ref[y * SUBGRID_SIDE : (y + 1) * SUBGRID_SIDE, :] = (v[y : y + 1, :] * u).astype(jnp.bfloat16)


WEIGHTS = [pltpu.VMEM((CELLS, SLOTS), jnp.bfloat16)]


def grid_total(blocks, weights_ref, total=None):
    for block in blocks:
        width = block.shape[0] - META
        fill_weights(block[width:, :], weights_ref)
        term = tensor_dot(weights_ref[...], block[:width, :], ((1,), (1,)))
        total = term if total is None else total + term
    return total


def grid_rows(blocks, dtype):
    count = len(blocks)

    def kernel(*refs):
        parts = []
        for (_, which), ref in zip(blocks, refs):
            parts += [ref] if which is None else [ref.at[j] for j in which]
        refs[-2][...] = grid_total(parts, refs[-1]).astype(dtype)

    return pl.pallas_call(
        kernel,
        in_specs=[VMEM_SPEC] * count,
        out_specs=VMEM_SPEC,
        out_shape=pltpu.VMEM((CELLS, blocks[0][0].shape[-2] - META), dtype),
        scratch_shapes=WEIGHTS,
        compiler_params=PARAMS,
        name="grid_rows",
    )(*[on_chip(x) for x, _ in blocks])


def grid_pieces(place, blocks, before=None):
    cells = CELLS // 4
    count = len(blocks)
    width = blocks[0][0].shape[-2] - META
    operands = [x for x, _ in blocks] + ([] if before is None else [before])

    def kernel(place_ref, *refs):
        piece_refs, total_ref, weights_ref = refs[-6:-2], refs[-2], refs[-1]
        parts = []
        for (_, which), ref in zip(blocks, refs):
            parts += [ref] if which is None else [ref.at[j] for j in which]
        total_ref[...] = grid_total(parts, weights_ref, None if before is None else refs[count][...])
        for d, piece_ref in enumerate(piece_refs):
            at = pl.ds(pl.multiple_of((place_ref[0] ^ d) * cells, cells), cells)
            piece_ref[...] = total_ref[at, :].astype(jnp.bfloat16)

    return pl.pallas_call(
        kernel,
        in_specs=[SMEM_SPEC] + [VMEM_SPEC] * len(operands),
        out_specs=[VMEM_SPEC] * 4,
        out_shape=[pltpu.VMEM((cells, width), jnp.bfloat16)] * 4,
        scratch_shapes=[pltpu.VMEM((CELLS, width), jnp.float32)] + WEIGHTS,
        compiler_params=PARAMS,
        name="grid_pieces",
    )(place, *[on_chip(x) for x in operands])


def stack(pieces):
    def kernel(*refs):
        for d, ref in enumerate(refs[:-1]):
            refs[-1][d] = ref[...]

    return pl.pallas_call(
        kernel,
        in_specs=[VMEM_SPEC] * len(pieces),
        out_specs=VMEM_SPEC,
        out_shape=pltpu.VMEM((len(pieces), *pieces[0].shape), pieces[0].dtype),
        compiler_params=PARAMS,
        name="stack",
    )(*[on_chip(x) for x in pieces])


def transform_matrix(length, width):
    n = np.arange(length)
    angle = (n[:, None] * n[None, :] % length) * (2.0 * np.pi / length)
    blocks = length // width
    cos = (np.cos(angle) / math.sqrt(length)).reshape(blocks, width, length)
    sin = (np.sin(angle) / math.sqrt(length)).reshape(blocks, width, length)
    whole = np.concatenate([cos, sin], axis=1)
    high = whole.astype(jnp.bfloat16)
    low = (whole - high.astype(np.float64)).astype(jnp.bfloat16)
    return high, low


def transform_kernel(place_ref, x0_ref, x1_ref, x2_ref, x3_ref, y0_ref, y_ref, high_ref, low_ref, out_ref):
    real = imag = None
    for d, ref in enumerate((x0_ref, x1_ref, x2_ref, x3_ref)):
        block = place_ref[0] ^ d
        more = y0_ref[...] if d == 0 else y_ref[d - 1]
        x = (ref[...].astype(jnp.float32) + more.astype(jnp.float32)).astype(jnp.bfloat16)
        width = x.shape[1] // 2
        turned = jnp.concatenate([x[:, width:], -x[:, :width]], axis=1)
        for matrix in (high_ref[block], low_ref[block]):
            a = tensor_dot(x, matrix, ((1,), (0,)))
            b = tensor_dot(turned, matrix, ((1,), (0,)))
            real = a if real is None else real + a
            imag = b if imag is None else imag + b
    out_ref[:, 0, :] = real
    out_ref[:, 1, :] = imag


def transform(place, pieces, first, rest, high, low):
    return pl.pallas_call(
        transform_kernel,
        in_specs=[SMEM_SPEC] + [VMEM_SPEC] * 8,
        out_specs=VMEM_SPEC,
        out_shape=jax.ShapeDtypeStruct((pieces[0].shape[0], 2, high.shape[2]), jnp.float32),
        compiler_params=PARAMS,
        name="transform",
    )(place, *[on_chip(x) for x in (*pieces, first, rest, high, low)])


def on_device_small(visibilities, pair_patch_number, baseline_kernel_taps, kernel_start_cells):
    rows_here, parts_count, channels = visibilities.shape
    patch = pair_patch_number.reshape(rows_here // 128, 128)
    place = lax.axis_index("chan").astype(jnp.int32).reshape(1)
    uv = lax.axis_index("uv").astype(jnp.int32).reshape(1)

    def send(block, pairs, j=0):
        return lax.ppermute(block, "uv", [(2 * a + c, 2 * b + (c ^ j)) for a, b in pairs for c in range(2)])

    def swap(block):
        return lax.ppermute(block, "uv", [(u, u ^ 1) for u in range(8)])

    def exchange(pieces):
        return [pieces[0]] + [lax.ppermute(pieces[d], "chan", [(c, c ^ d) for c in range(4)]) for d in range(1, 4)]

    first0, first1, first, columns, rank = sort_first(
        uv, patch, baseline_kernel_taps.T, kernel_start_cells.T, visibilities
    )
    columns2 = swap(columns)
    far_in = [send(first0, [(0, 1), (3, 2)]), send(first1, [(0, 1), (3, 2)], 1)]
    near_in = send(first, [(1, 2), (2, 1)])
    second, rank2 = sort_second(uv, rank, columns, columns2)
    second_in = send(second, [(0, 2), (3, 1), (1, 0), (2, 3)])
    third, own = sort_rest(uv, rank, rank2, columns, columns2)
    sums = exchange(grid_pieces(place, [(third, (0, 1)), (far_in[0], None), (far_in[1], None)]))
    onward = [(0, 1), (3, 2), (1, 3), (2, 0)]
    sum_first, sum_rest = send(sums[0], onward), send(stack(sums[1:]), onward)
    near_in, own, _ = lax.optimization_barrier((near_in, own, sums[0]))
    grid = grid_rows([(own, (0, 1)), (near_in, (0,)), (swap(near_in[1]), None)], jnp.float32)
    second_in, grid = lax.optimization_barrier((second_in, grid))
    pieces = exchange(grid_pieces(place, [(second_in, (0, 1))], grid))
    high, low = transform_matrix(4 * channels, channels)
    return transform(place, pieces, sum_first, sum_rest, jnp.asarray(high), jnp.asarray(low))[None]


def kernel_rows(taps_float, offsets_float, cells_side):
    cell_index = jnp.arange(cells_side, dtype=jnp.float32)
    tap_index = jnp.arange(KERNEL_TAPS, dtype=jnp.float32)

    def one_axis(tap_values, opening_pixel):
        matches = (
            cell_index[None, None, :] == opening_pixel[:, None, None] + tap_index[None, :, None]
        ).astype(jnp.float32)
        return jnp.sum(tap_values[:, :, None] * matches, axis=1)

    return (
        one_axis(taps_float[:, :KERNEL_TAPS], offsets_float[:, 0]),
        one_axis(taps_float[:, KERNEL_TAPS : 2 * KERNEL_TAPS], offsets_float[:, 1]),
    )


def angle_table(row_count, col_count, period):
    row_ids = jnp.arange(row_count, dtype=jnp.int32)[:, None]
    col_ids = jnp.arange(col_count, dtype=jnp.int32)[None, :]
    angles = (row_ids * col_ids % period).astype(jnp.float32) * (2.0 * math.pi / period)
    return (jnp.cos(angles), jnp.sin(angles))


def delay_transform(pencil_data):
    leading, cell_count, parts_count, length = pencil_data.shape
    inner_len = 128
    outer_len = length // inner_len
    fine = lax.Precision.HIGH
    wide = jnp.float32
    values = pencil_data.reshape(leading * cell_count, parts_count, outer_len, inner_len)
    real_part = values[:, 0]
    imag_part = values[:, 1]
    cos_outer, sin_outer = angle_table(outer_len, outer_len, outer_len)
    first_real = jnp.einsum(
        "kn,mnj->mkj", cos_outer, real_part, precision=fine, preferred_element_type=wide
    ) + jnp.einsum("kn,mnj->mkj", sin_outer, imag_part, precision=fine, preferred_element_type=wide)
    first_imag = jnp.einsum(
        "kn,mnj->mkj", cos_outer, imag_part, precision=fine, preferred_element_type=wide
    ) - jnp.einsum("kn,mnj->mkj", sin_outer, real_part, precision=fine, preferred_element_type=wide)
    cos_twist, sin_twist = angle_table(outer_len, inner_len, length)
    twisted_real = first_real * cos_twist + first_imag * sin_twist
    twisted_imag = first_imag * cos_twist - first_real * sin_twist
    cos_inner, sin_inner = angle_table(inner_len, inner_len, inner_len)
    final_real = jnp.einsum("mkn,nq->mqk", twisted_real, cos_inner, precision=fine) + jnp.einsum(
        "mkn,nq->mqk", twisted_imag, sin_inner, precision=fine
    )
    final_imag = jnp.einsum("mkn,nq->mqk", twisted_imag, cos_inner, precision=fine) - jnp.einsum(
        "mkn,nq->mqk", twisted_real, sin_inner, precision=fine
    )
    scaling = 1.0 / math.sqrt(length)
    stacked = (
        jnp.stack([final_real.reshape(-1, length), final_imag.reshape(-1, length)], axis=1)
        * scaling
    )
    return stacked.reshape(leading, cell_count, parts_count, length)


def on_device_large(visibilities, pair_patch_number, baseline_kernel_taps, kernel_start_cells):
    rows_here, parts_count, frequency_bins = visibilities.shape
    uv_devices = lax.axis_size("uv")
    capacity = 2 * rows_here // uv_devices
    slot_count = uv_devices * capacity
    flat_layout = visibilities.reshape(rows_here, parts_count * frequency_bins)
    subgrid_list = pair_patch_number[:, 0]
    member = (subgrid_list[:, None] == jnp.arange(uv_devices, dtype=jnp.int32)[None, :]).astype(
        jnp.int32
    )
    preceding = jnp.sum((jnp.cumsum(member, axis=0) - member) * member, axis=1)
    target = subgrid_list * capacity + preceding
    vis_buffer = (
        jnp.zeros((slot_count, parts_count * frequency_bins), jnp.bfloat16)
        .at[target]
        .set(flat_layout)
    )
    vis_buffer = vis_buffer.reshape(uv_devices, capacity, parts_count * frequency_bins)
    u_rows, v_rows = kernel_rows(
        baseline_kernel_taps.astype(jnp.float32),
        kernel_start_cells.astype(jnp.float32),
        SUBGRID_SIDE,
    )
    payload = jnp.concatenate([u_rows, v_rows], axis=1).astype(jnp.bfloat16)
    payload_buffer = jnp.zeros((slot_count, 2 * SUBGRID_SIDE), jnp.bfloat16).at[target].set(payload)
    got_vis, got_payload = (
        lax.all_to_all(vis_buffer, "uv", split_axis=0, concat_axis=0, tiled=True),
        lax.all_to_all(
            payload_buffer.reshape(uv_devices, capacity, 2 * SUBGRID_SIDE),
            "uv",
            split_axis=0,
            concat_axis=0,
            tiled=True,
        ),
    )

    def kernels(payload_block):
        widened = payload_block.astype(jnp.float32)
        return (widened[:, :SUBGRID_SIDE], widened[:, SUBGRID_SIDE:])

    got_vis = got_vis.reshape(slot_count, parts_count * frequency_bins)
    got_payload = got_payload.reshape(slot_count, -1)
    stride = math.gcd(slot_count, 256)
    turn_count = slot_count // stride

    def accumulate(counter, accumulated):
        starting = counter * stride
        vis_block = lax.dynamic_slice_in_dim(got_vis, starting, stride, 0)
        payload_block = lax.dynamic_slice_in_dim(got_payload, starting, stride, 0)
        u_block, v_block = kernels(payload_block)
        weights = (
            (v_block[:, :, None] * u_block[:, None, :])
            .reshape(stride, SUBGRID_SIDE * SUBGRID_SIDE)
            .astype(jnp.bfloat16)
        )
        return accumulated + lax.dot_general(
            weights, vis_block, (((0,), (0,)), ((), ())), preferred_element_type=jnp.float32
        )

    gridded = lax.fori_loop(
        0,
        turn_count,
        accumulate,
        jnp.zeros((SUBGRID_SIDE * SUBGRID_SIDE, parts_count * frequency_bins), jnp.float32),
    )
    gridded = gridded.astype(jnp.bfloat16)
    chan_devices = lax.axis_size("chan")
    pieces = gridded.reshape(
        chan_devices, SUBGRID_SIDE * SUBGRID_SIDE // chan_devices, parts_count, frequency_bins
    )
    return delay_transform(lax.all_to_all(pieces, "chan", split_axis=0, concat_axis=3, tiled=True))


def solution(mesh):
    in_specs = (P("uv", None, "chan"), P("uv", None), P("uv", None), P("uv", None))
    out_specs = P("uv", "chan", None, None)
    small = mesh.shape["uv"] == 8 and mesh.shape["chan"] == 4
    return jax.shard_map(
        on_device_small if small else on_device_large,
        mesh=mesh,
        in_specs=in_specs,
        out_specs=out_specs,
        check_vma=False,
    )
```

```python
import functools
import math

import jax
import jax.numpy as jnp
import numpy as np
from jax import lax
from jax.experimental import pallas as pl
from jax.experimental.pallas import tpu as pltpu
from jax.sharding import PartitionSpec as P

SUBGRID_SIDE = 32
KERNEL_TAPS = 8
CELLS = SUBGRID_SIDE * SUBGRID_SIDE
HALF = 256
SLOTS = 2 * HALF
META = 24
PATCH = 2
RANK = 3
VMEM_LIMIT = 24 << 20
VMEM_SPEC = pl.BlockSpec(memory_space=pltpu.VMEM)
SMEM_SPEC = pl.BlockSpec(memory_space=pltpu.SMEM)
PARAMS = pltpu.CompilerParams(vmem_limit_bytes=VMEM_LIMIT)


def on_chip(x):
    return pltpu.with_memory_space_constraint(x, pltpu.VMEM)


def tensor_dot(a, b, dims):
    return lax.dot_general(a, b, (dims, ((), ())), preferred_element_type=jnp.float32)


def place_rows(patch):
    groups, lanes = patch.shape
    members = jnp.concatenate([(patch == s).astype(jnp.float32) for s in range(8)], axis=0).astype(jnp.bfloat16)
    row = lax.broadcasted_iota(jnp.int32, (lanes, lanes), 0)
    col = lax.broadcasted_iota(jnp.int32, (lanes, lanes), 1)
    before = (row < col).astype(jnp.float32).astype(jnp.bfloat16)
    ahead = tensor_dot(members, before, ((1,), (0,)))
    totals = tensor_dot(members, jnp.ones((lanes, lanes), jnp.bfloat16), ((1,), (0,)))
    r = lax.broadcasted_iota(jnp.int32, (8 * groups, 8 * groups), 0)
    c = lax.broadcasted_iota(jnp.int32, (8 * groups, 8 * groups), 1)
    earlier = ((c < r) & (c // groups == r // groups)).astype(jnp.float32).astype(jnp.bfloat16)
    rank_all = ahead + tensor_dot(earlier, totals.astype(jnp.bfloat16), ((1,), (0,)))
    rank = jnp.zeros((groups, lanes), jnp.float32)
    for s in range(8):
        rank = jnp.where(patch == s, rank_all[s * groups : (s + 1) * groups], rank)
    return rank


def sort_into(target, columns_ref, out_ref):
    lanes = 128
    groups = columns_ref.shape[1] // lanes
    at = columns_ref.shape[0] - META + 2 * KERNEL_TAPS
    data = columns_ref[at : at + META - 2 * KERNEL_TAPS, :].astype(jnp.float32)
    patch = data[PATCH : PATCH + 1, :]
    rank = data[RANK : RANK + 1, :] * HALF + data[RANK + 1 : RANK + 2, :]
    mine = patch == target.astype(jnp.float32)
    slot = lax.broadcasted_iota(jnp.int32, (HALF, lanes), 0).astype(jnp.float32).astype(jnp.bfloat16)
    slot = slot.reshape(HALF // 16, 16, lanes)
    one = jnp.ones((), jnp.bfloat16)
    zero = jnp.zeros((), jnp.bfloat16)

    def selection(h):
        key = jnp.where(mine, rank - h * HALF, -1.0)
        key = jnp.where(key < HALF, key, -1.0)
        pieces = []
        for k in range(groups):
            k16 = jnp.broadcast_to(key[:, k * lanes : (k + 1) * lanes], (16, lanes)).astype(jnp.bfloat16)
            pieces.append(jnp.where(slot == k16[None], one, zero).reshape(HALF, lanes))
        return jnp.concatenate(pieces, axis=1)

    select = jnp.concatenate([selection(0), selection(1)], axis=0)
    out_ref[...] = tensor_dot(columns_ref[...], select, ((1,), (1,))).astype(jnp.bfloat16)


def prepare(patch, taps, starts, vis):
    rows, parts, channels = vis.shape
    width = parts * channels

    def kernel(
        patch_hbm, taps_hbm, starts_hbm, vis_hbm, columns_ref,
        patch_ref, taps_ref, starts_ref, vis_ref, sems,
    ):
        copies = [
            pltpu.make_async_copy(patch_hbm, patch_ref, sems.at[0]),
            pltpu.make_async_copy(vis_hbm, vis_ref, sems.at[1]),
            pltpu.make_async_copy(taps_hbm, taps_ref, sems.at[2]),
            pltpu.make_async_copy(starts_hbm, starts_ref, sems.at[3]),
        ]
        for copy in copies:
            copy.start()
        copies[0].wait()
        patch = patch_ref[...]
        rank = place_rows(patch)
        high = jnp.floor(rank * (1.0 / HALF))
        copies[2].wait()
        copies[3].wait()

        def row_of(x):
            return jnp.concatenate([x[k : k + 1, :] for k in range(x.shape[0])], axis=1)

        columns_ref[width:, :] = jnp.concatenate(
            [
                taps_ref[...].astype(jnp.float32),
                starts_ref[...].astype(jnp.float32),
                row_of(patch.astype(jnp.float32)),
                row_of(high),
                row_of(rank - high * HALF),
                jnp.zeros((META - 2 * KERNEL_TAPS - 5, rows), jnp.float32),
            ],
            axis=0,
        ).astype(jnp.bfloat16)
        copies[1].wait()
        columns_ref[:width, :] = vis_ref[...].reshape(rows, width).T

    in_hbm = [pltpu.with_memory_space_constraint(x, pltpu.HBM) for x in (patch, taps, starts, vis)]
    return pl.pallas_call(
        kernel,
        in_specs=[pl.BlockSpec(memory_space=pl.ANY)] * 4,
        out_specs=VMEM_SPEC,
        out_shape=pltpu.VMEM((width + META, rows), jnp.bfloat16),
        scratch_shapes=[pltpu.VMEM(x.shape, x.dtype) for x in (patch, taps, starts, vis)]
        + [pltpu.SemaphoreType.DMA((4,))],
        compiler_params=PARAMS,
        name="prepare",
    )(*in_hbm)


def at_ends(z, end, middle):
    return jnp.where((z == 0) | (z == 3), end, middle)


def sort_pairs(which, uv, columns, columns2):
    def kernel(uv_ref, columns_ref, columns2_ref, *pair_refs):
        z = uv_ref[0] // 2
        for target_z, ref in zip(which, pair_refs):
            target = 2 * target_z(z) + uv_ref[0] % 2
            sort_into(target, columns_ref, ref.at[0])
            sort_into(target, columns2_ref, ref.at[1])

    return pl.pallas_call(
        kernel,
        in_specs=[SMEM_SPEC] + [VMEM_SPEC] * 2,
        out_specs=[VMEM_SPEC] * len(which),
        out_shape=[pltpu.VMEM((2, columns.shape[0], SLOTS), jnp.bfloat16)] * len(which),
        compiler_params=PARAMS,
        name="sort_pairs",
    )(uv, on_chip(columns), on_chip(columns2))


def spread(taps, start):
    cell = lax.broadcasted_iota(jnp.int32, (SUBGRID_SIDE, SLOTS), 0).astype(jnp.float32)
    offset = cell - start
    out = jnp.zeros((SUBGRID_SIDE, SLOTS), jnp.float32)
    for i in range(KERNEL_TAPS):
        out = jnp.where(offset == i, taps[i : i + 1, :], out)
    return out


def fill_weights(meta, weights_ref):
    meta = meta.astype(jnp.float32)
    u = spread(meta[:KERNEL_TAPS], meta[2 * KERNEL_TAPS : 2 * KERNEL_TAPS + 1])
    v = spread(meta[KERNEL_TAPS : 2 * KERNEL_TAPS], meta[2 * KERNEL_TAPS + 1 : 2 * KERNEL_TAPS + 2])
    for y in range(SUBGRID_SIDE):
        weights_ref[y * SUBGRID_SIDE : (y + 1) * SUBGRID_SIDE, :] = (v[y : y + 1, :] * u).astype(jnp.bfloat16)


WEIGHTS = [pltpu.VMEM((CELLS, SLOTS), jnp.bfloat16)]


def grid_total(blocks, weights_ref, total=None):
    for block in blocks:
        width = block.shape[0] - META
        fill_weights(block[width:, :], weights_ref)
        term = tensor_dot(weights_ref[...], block[:width, :], ((1,), (1,)))
        total = term if total is None else total + term
    return total


def grid_rows(blocks, dtype):
    count = len(blocks)

    def kernel(*refs):
        parts = []
        for (_, which), ref in zip(blocks, refs):
            parts += [ref] if which is None else [ref.at[j] for j in which]
        refs[-2][...] = grid_total(parts, refs[-1]).astype(dtype)

    return pl.pallas_call(
        kernel,
        in_specs=[VMEM_SPEC] * count,
        out_specs=VMEM_SPEC,
        out_shape=pltpu.VMEM((CELLS, blocks[0][0].shape[-2] - META), dtype),
        scratch_shapes=WEIGHTS,
        compiler_params=PARAMS,
        name="grid_rows",
    )(*[on_chip(x) for x, _ in blocks])


def grid_pieces(place, blocks, before=None):
    cells = CELLS // 4
    count = len(blocks)
    width = blocks[0][0].shape[-2] - META
    operands = [x for x, _ in blocks] + ([] if before is None else [before])

    def kernel(place_ref, *refs):
        piece_refs, total_ref, weights_ref = refs[-6:-2], refs[-2], refs[-1]
        parts = []
        for (_, which), ref in zip(blocks, refs):
            parts += [ref] if which is None else [ref.at[j] for j in which]
        total_ref[...] = grid_total(parts, weights_ref, None if before is None else refs[count][...])
        for d, piece_ref in enumerate(piece_refs):
            at = pl.ds(pl.multiple_of((place_ref[0] ^ d) * cells, cells), cells)
            piece_ref[...] = total_ref[at, :].astype(jnp.bfloat16)

    return pl.pallas_call(
        kernel,
        in_specs=[SMEM_SPEC] + [VMEM_SPEC] * len(operands),
        out_specs=[VMEM_SPEC] * 4,
        out_shape=[pltpu.VMEM((cells, width), jnp.bfloat16)] * 4,
        scratch_shapes=[pltpu.VMEM((CELLS, width), jnp.float32)] + WEIGHTS,
        compiler_params=PARAMS,
        name="grid_pieces",
    )(place, *[on_chip(x) for x in operands])


def stack(pieces):
    def kernel(*refs):
        for d, ref in enumerate(refs[:-1]):
            refs[-1][d] = ref[...]

    return pl.pallas_call(
        kernel,
        in_specs=[VMEM_SPEC] * len(pieces),
        out_specs=VMEM_SPEC,
        out_shape=pltpu.VMEM((len(pieces), *pieces[0].shape), pieces[0].dtype),
        compiler_params=PARAMS,
        name="stack",
    )(*[on_chip(x) for x in pieces])


def transform_matrix(length, width):
    n = np.arange(length)
    angle = (n[:, None] * n[None, :] % length) * (2.0 * np.pi / length)
    blocks = length // width
    cos = (np.cos(angle) / math.sqrt(length)).reshape(blocks, width, length)
    sin = (np.sin(angle) / math.sqrt(length)).reshape(blocks, width, length)
    whole = np.concatenate([cos, sin], axis=1)
    high = whole.astype(jnp.bfloat16)
    low = (whole - high.astype(np.float64)).astype(jnp.bfloat16)
    return high, low


def transform_kernel(place_ref, x0_ref, x1_ref, x2_ref, x3_ref, late_ref, high_ref, low_ref, out_ref):
    total = None
    for d, ref in enumerate((x0_ref, x1_ref, x2_ref, x3_ref)):
        block = place_ref[0] ^ d
        x = (ref[...].astype(jnp.float32) + late_ref[d].astype(jnp.float32)).astype(jnp.bfloat16)
        width = x.shape[1] // 2
        turned = jnp.concatenate([x[:, width:], -x[:, :width]], axis=1)
        x = jnp.concatenate([x, turned], axis=0)
        for matrix in (high_ref[block], low_ref[block]):
            term = tensor_dot(x, matrix, ((1,), (0,)))
            total = term if total is None else total + term
    cells = out_ref.shape[0]
    out_ref[:, 0, :] = total[:cells]
    out_ref[:, 1, :] = total[cells:]


def transform(place, pieces, late, high, low):
    return pl.pallas_call(
        transform_kernel,
        in_specs=[SMEM_SPEC] + [VMEM_SPEC] * 7,
        out_specs=VMEM_SPEC,
        out_shape=jax.ShapeDtypeStruct((pieces[0].shape[0], 2, high.shape[2]), jnp.float32),
        compiler_params=PARAMS,
        name="transform",
    )(place, *[on_chip(x) for x in (*pieces, late, high, low)])


def on_device_small(visibilities, pair_patch_number, baseline_kernel_taps, kernel_start_cells):
    rows_here, parts_count, channels = visibilities.shape
    patch = pair_patch_number.reshape(rows_here // 128, 128)
    place = lax.axis_index("chan").astype(jnp.int32).reshape(1)
    uv = lax.axis_index("uv").astype(jnp.int32).reshape(1)

    def send(block, pairs, j=0):
        return lax.ppermute(block, "uv", [(2 * a + c, 2 * b + (c ^ j)) for a, b in pairs for c in range(2)])

    def swap(block):
        return lax.ppermute(block, "uv", [(u, u ^ 1) for u in range(8)])

    def exchange(pieces):
        return [pieces[0]] + [lax.ppermute(pieces[d], "chan", [(c, c ^ d) for c in range(4)]) for d in range(1, 4)]

    columns = prepare(patch, baseline_kernel_taps.T, kernel_start_cells.T, visibilities)
    columns2 = swap(columns)
    (first,) = sort_pairs([lambda z: 3 - z], uv, columns, columns2)
    far_in = send(first, [(0, 1), (3, 2)])
    near_in = send(first, [(1, 2), (2, 1)])
    (second,) = sort_pairs([lambda z: at_ends(z, (3 - z) ^ 1, z ^ 1)], uv, columns, columns2)
    second_in = send(second, [(0, 2), (3, 1), (1, 0), (2, 3)])
    third, own = sort_pairs([lambda z: at_ends(z, z ^ 1, (3 - z) ^ 1), lambda z: z], uv, columns, columns2)
    pair = (0, 1)
    sums = grid_rows([(third, pair)], jnp.float32)
    far_in, sums = lax.optimization_barrier((far_in, sums))
    sums = exchange(grid_pieces(place, [(far_in, pair)], sums))
    onward = [(0, 1), (3, 2), (1, 3), (2, 0)]
    late = send(stack(sums), onward)
    near_in, own, _ = lax.optimization_barrier((near_in, own, sums[0]))
    grid = grid_rows([(own, pair), (near_in, pair)], jnp.float32)
    second_in, grid = lax.optimization_barrier((second_in, grid))
    pieces = exchange(grid_pieces(place, [(second_in, pair)], grid))
    high, low = transform_matrix(4 * channels, channels)
    return transform(place, pieces, late, jnp.asarray(high), jnp.asarray(low))[None]


def kernel_rows(taps_float, offsets_float, cells_side):
    cell_index = jnp.arange(cells_side, dtype=jnp.float32)
    tap_index = jnp.arange(KERNEL_TAPS, dtype=jnp.float32)

    def one_axis(tap_values, opening_pixel):
        matches = (
            cell_index[None, None, :] == opening_pixel[:, None, None] + tap_index[None, :, None]
        ).astype(jnp.float32)
        return jnp.sum(tap_values[:, :, None] * matches, axis=1)

    return (
        one_axis(taps_float[:, :KERNEL_TAPS], offsets_float[:, 0]),
        one_axis(taps_float[:, KERNEL_TAPS : 2 * KERNEL_TAPS], offsets_float[:, 1]),
    )


def angle_table(row_count, col_count, period):
    row_ids = jnp.arange(row_count, dtype=jnp.int32)[:, None]
    col_ids = jnp.arange(col_count, dtype=jnp.int32)[None, :]
    angles = (row_ids * col_ids % period).astype(jnp.float32) * (2.0 * math.pi / period)
    return (jnp.cos(angles), jnp.sin(angles))


def delay_transform(pencil_data):
    leading, cell_count, parts_count, length = pencil_data.shape
    inner_len = 128
    outer_len = length // inner_len
    fine = lax.Precision.HIGH
    wide = jnp.float32
    values = pencil_data.reshape(leading * cell_count, parts_count, outer_len, inner_len)
    real_part = values[:, 0]
    imag_part = values[:, 1]
    cos_outer, sin_outer = angle_table(outer_len, outer_len, outer_len)
    first_real = jnp.einsum(
        "kn,mnj->mkj", cos_outer, real_part, precision=fine, preferred_element_type=wide
    ) + jnp.einsum("kn,mnj->mkj", sin_outer, imag_part, precision=fine, preferred_element_type=wide)
    first_imag = jnp.einsum(
        "kn,mnj->mkj", cos_outer, imag_part, precision=fine, preferred_element_type=wide
    ) - jnp.einsum("kn,mnj->mkj", sin_outer, real_part, precision=fine, preferred_element_type=wide)
    cos_twist, sin_twist = angle_table(outer_len, inner_len, length)
    twisted_real = first_real * cos_twist + first_imag * sin_twist
    twisted_imag = first_imag * cos_twist - first_real * sin_twist
    cos_inner, sin_inner = angle_table(inner_len, inner_len, inner_len)
    final_real = jnp.einsum("mkn,nq->mqk", twisted_real, cos_inner, precision=fine) + jnp.einsum(
        "mkn,nq->mqk", twisted_imag, sin_inner, precision=fine
    )
    final_imag = jnp.einsum("mkn,nq->mqk", twisted_imag, cos_inner, precision=fine) - jnp.einsum(
        "mkn,nq->mqk", twisted_real, sin_inner, precision=fine
    )
    scaling = 1.0 / math.sqrt(length)
    stacked = (
        jnp.stack([final_real.reshape(-1, length), final_imag.reshape(-1, length)], axis=1)
        * scaling
    )
    return stacked.reshape(leading, cell_count, parts_count, length)


def on_device_large(visibilities, pair_patch_number, baseline_kernel_taps, kernel_start_cells):
    rows_here, parts_count, frequency_bins = visibilities.shape
    uv_devices = lax.axis_size("uv")
    capacity = 2 * rows_here // uv_devices
    slot_count = uv_devices * capacity
    flat_layout = visibilities.reshape(rows_here, parts_count * frequency_bins)
    subgrid_list = pair_patch_number[:, 0]
    member = (subgrid_list[:, None] == jnp.arange(uv_devices, dtype=jnp.int32)[None, :]).astype(
        jnp.int32
    )
    preceding = jnp.sum((jnp.cumsum(member, axis=0) - member) * member, axis=1)
    target = subgrid_list * capacity + preceding
    vis_buffer = (
        jnp.zeros((slot_count, parts_count * frequency_bins), jnp.bfloat16)
        .at[target]
        .set(flat_layout)
    )
    vis_buffer = vis_buffer.reshape(uv_devices, capacity, parts_count * frequency_bins)
    u_rows, v_rows = kernel_rows(
        baseline_kernel_taps.astype(jnp.float32),
        kernel_start_cells.astype(jnp.float32),
        SUBGRID_SIDE,
    )
    payload = jnp.concatenate([u_rows, v_rows], axis=1).astype(jnp.bfloat16)
    payload_buffer = jnp.zeros((slot_count, 2 * SUBGRID_SIDE), jnp.bfloat16).at[target].set(payload)
    got_vis, got_payload = (
        lax.all_to_all(vis_buffer, "uv", split_axis=0, concat_axis=0, tiled=True),
        lax.all_to_all(
            payload_buffer.reshape(uv_devices, capacity, 2 * SUBGRID_SIDE),
            "uv",
            split_axis=0,
            concat_axis=0,
            tiled=True,
        ),
    )

    def kernels(payload_block):
        widened = payload_block.astype(jnp.float32)
        return (widened[:, :SUBGRID_SIDE], widened[:, SUBGRID_SIDE:])

    got_vis = got_vis.reshape(slot_count, parts_count * frequency_bins)
    got_payload = got_payload.reshape(slot_count, -1)
    stride = math.gcd(slot_count, 256)
    turn_count = slot_count // stride

    def accumulate(counter, accumulated):
        starting = counter * stride
        vis_block = lax.dynamic_slice_in_dim(got_vis, starting, stride, 0)
        payload_block = lax.dynamic_slice_in_dim(got_payload, starting, stride, 0)
        u_block, v_block = kernels(payload_block)
        weights = (
            (v_block[:, :, None] * u_block[:, None, :])
            .reshape(stride, SUBGRID_SIDE * SUBGRID_SIDE)
            .astype(jnp.bfloat16)
        )
        return accumulated + lax.dot_general(
            weights, vis_block, (((0,), (0,)), ((), ())), preferred_element_type=jnp.float32
        )

    gridded = lax.fori_loop(
        0,
        turn_count,
        accumulate,
        jnp.zeros((SUBGRID_SIDE * SUBGRID_SIDE, parts_count * frequency_bins), jnp.float32),
    )
    gridded = gridded.astype(jnp.bfloat16)
    chan_devices = lax.axis_size("chan")
    pieces = gridded.reshape(
        chan_devices, SUBGRID_SIDE * SUBGRID_SIDE // chan_devices, parts_count, frequency_bins
    )
    return delay_transform(lax.all_to_all(pieces, "chan", split_axis=0, concat_axis=3, tiled=True))


def solution(mesh):
    in_specs = (P("uv", None, "chan"), P("uv", None), P("uv", None), P("uv", None))
    out_specs = P("uv", "chan", None, None)
    small = mesh.shape["uv"] == 8 and mesh.shape["chan"] == 4
    return jax.shard_map(
        on_device_small if small else on_device_large,
        mesh=mesh,
        in_specs=in_specs,
        out_specs=out_specs,
        check_vma=False,
    )
```

```python
import functools
import math

import jax
import jax.numpy as jnp
import numpy as np
from jax import lax
from jax.experimental import pallas as pl
from jax.experimental.pallas import tpu as pltpu
from jax.sharding import PartitionSpec as P

SUBGRID_SIDE = 32
KERNEL_TAPS = 8
CELLS = SUBGRID_SIDE * SUBGRID_SIDE
HALF = 256
SLOTS = 2 * HALF
META = 24
PATCH = 2
RANK = 3
VMEM_LIMIT = 24 << 20
VMEM_SPEC = pl.BlockSpec(memory_space=pltpu.VMEM)
SMEM_SPEC = pl.BlockSpec(memory_space=pltpu.SMEM)
PARAMS = pltpu.CompilerParams(vmem_limit_bytes=VMEM_LIMIT)


def on_chip(x):
    return pltpu.with_memory_space_constraint(x, pltpu.VMEM)


def tensor_dot(a, b, dims):
    return lax.dot_general(a, b, (dims, ((), ())), preferred_element_type=jnp.float32)


def place_rows(patch):
    groups, lanes = patch.shape
    members = jnp.concatenate([(patch == s).astype(jnp.float32) for s in range(8)], axis=0).astype(jnp.bfloat16)
    row = lax.broadcasted_iota(jnp.int32, (lanes, lanes), 0)
    col = lax.broadcasted_iota(jnp.int32, (lanes, lanes), 1)
    before = (row < col).astype(jnp.float32).astype(jnp.bfloat16)
    ahead = tensor_dot(members, before, ((1,), (0,)))
    totals = tensor_dot(members, jnp.ones((lanes, lanes), jnp.bfloat16), ((1,), (0,)))
    r = lax.broadcasted_iota(jnp.int32, (8 * groups, 8 * groups), 0)
    c = lax.broadcasted_iota(jnp.int32, (8 * groups, 8 * groups), 1)
    earlier = ((c < r) & (c // groups == r // groups)).astype(jnp.float32).astype(jnp.bfloat16)
    rank_all = ahead + tensor_dot(earlier, totals.astype(jnp.bfloat16), ((1,), (0,)))
    rank = jnp.zeros((groups, lanes), jnp.float32)
    for s in range(8):
        rank = jnp.where(patch == s, rank_all[s * groups : (s + 1) * groups], rank)
    return rank


def sort_into(target, columns_ref, out_ref):
    lanes = 128
    groups = columns_ref.shape[1] // lanes
    at = columns_ref.shape[0] - META + 2 * KERNEL_TAPS
    data = columns_ref[at : at + META - 2 * KERNEL_TAPS, :].astype(jnp.float32)
    patch = data[PATCH : PATCH + 1, :]
    rank = data[RANK : RANK + 1, :] * HALF + data[RANK + 1 : RANK + 2, :]
    mine = patch == target.astype(jnp.float32)
    slot = lax.broadcasted_iota(jnp.int32, (HALF, lanes), 0).astype(jnp.float32).astype(jnp.bfloat16)
    slot = slot.reshape(HALF // 16, 16, lanes)
    one = jnp.ones((), jnp.bfloat16)
    zero = jnp.zeros((), jnp.bfloat16)

    def selection(h):
        key = jnp.where(mine, rank - h * HALF, -1.0)
        key = jnp.where(key < HALF, key, -1.0)
        pieces = []
        for k in range(groups):
            k16 = jnp.broadcast_to(key[:, k * lanes : (k + 1) * lanes], (16, lanes)).astype(jnp.bfloat16)
            pieces.append(jnp.where(slot == k16[None], one, zero).reshape(HALF, lanes))
        return jnp.concatenate(pieces, axis=1)

    select = jnp.concatenate([selection(0), selection(1)], axis=0)
    out_ref[...] = tensor_dot(columns_ref[...], select, ((1,), (1,))).astype(jnp.bfloat16)


def prepare(patch, taps, starts, vis):
    rows, parts, channels = vis.shape
    width = parts * channels

    def kernel(
        patch_hbm, taps_hbm, starts_hbm, vis_hbm, columns_ref,
        patch_ref, taps_ref, starts_ref, vis_ref, sems,
    ):
        copies = [
            pltpu.make_async_copy(patch_hbm, patch_ref, sems.at[0]),
            pltpu.make_async_copy(vis_hbm, vis_ref, sems.at[1]),
            pltpu.make_async_copy(taps_hbm, taps_ref, sems.at[2]),
            pltpu.make_async_copy(starts_hbm, starts_ref, sems.at[3]),
        ]
        for copy in copies:
            copy.start()
        copies[0].wait()
        patch = patch_ref[...]
        rank = place_rows(patch)
        high = jnp.floor(rank * (1.0 / HALF))
        copies[2].wait()
        copies[3].wait()

        def row_of(x):
            return jnp.concatenate([x[k : k + 1, :] for k in range(x.shape[0])], axis=1)

        columns_ref[width:, :] = jnp.concatenate(
            [
                taps_ref[...].astype(jnp.float32),
                starts_ref[...].astype(jnp.float32),
                row_of(patch.astype(jnp.float32)),
                row_of(high),
                row_of(rank - high * HALF),
                jnp.zeros((META - 2 * KERNEL_TAPS - 5, rows), jnp.float32),
            ],
            axis=0,
        ).astype(jnp.bfloat16)
        copies[1].wait()
        columns_ref[:width, :] = vis_ref[...].reshape(rows, width).T

    in_hbm = [pltpu.with_memory_space_constraint(x, pltpu.HBM) for x in (patch, taps, starts, vis)]
    return pl.pallas_call(
        kernel,
        in_specs=[pl.BlockSpec(memory_space=pl.ANY)] * 4,
        out_specs=VMEM_SPEC,
        out_shape=pltpu.VMEM((width + META, rows), jnp.bfloat16),
        scratch_shapes=[pltpu.VMEM(x.shape, x.dtype) for x in (patch, taps, starts, vis)]
        + [pltpu.SemaphoreType.DMA((4,))],
        compiler_params=PARAMS,
        name="prepare",
    )(*in_hbm)


def at_ends(z, end, middle):
    return jnp.where((z == 0) | (z == 3), end, middle)


def sort_pairs(which, uv, columns, columns2, after=()):
    count = len(which)

    def kernel(uv_ref, columns_ref, columns2_ref, *refs):
        z = uv_ref[0] // 2
        for target_z, ref in zip(which, refs[len(after) :]):
            target = 2 * target_z(z) + uv_ref[0] % 2
            sort_into(target, columns_ref, ref.at[0])
            sort_into(target, columns2_ref, ref.at[1])

    return pl.pallas_call(
        kernel,
        in_specs=[SMEM_SPEC] + [VMEM_SPEC] * (2 + len(after)),
        out_specs=[VMEM_SPEC] * count,
        out_shape=[pltpu.VMEM((2, columns.shape[0], SLOTS), jnp.bfloat16)] * count,
        compiler_params=PARAMS,
        name="sort_pairs",
    )(uv, *[on_chip(x) for x in (columns, columns2, *after)])


def spread(taps, start):
    cell = lax.broadcasted_iota(jnp.int32, (SUBGRID_SIDE, SLOTS), 0).astype(jnp.float32)
    offset = cell - start
    out = jnp.zeros((SUBGRID_SIDE, SLOTS), jnp.float32)
    for i in range(KERNEL_TAPS):
        out = jnp.where(offset == i, taps[i : i + 1, :], out)
    return out


def fill_weights(meta, weights_ref):
    meta = meta.astype(jnp.float32)
    u = spread(meta[:KERNEL_TAPS], meta[2 * KERNEL_TAPS : 2 * KERNEL_TAPS + 1])
    v = spread(meta[KERNEL_TAPS : 2 * KERNEL_TAPS], meta[2 * KERNEL_TAPS + 1 : 2 * KERNEL_TAPS + 2])
    for y in range(SUBGRID_SIDE):
        weights_ref[y * SUBGRID_SIDE : (y + 1) * SUBGRID_SIDE, :] = (v[y : y + 1, :] * u).astype(jnp.bfloat16)


WEIGHTS = [pltpu.VMEM((CELLS, SLOTS), jnp.bfloat16)]


def grid_total(blocks, weights_ref, total=None):
    for block in blocks:
        width = block.shape[0] - META
        fill_weights(block[width:, :], weights_ref)
        term = tensor_dot(weights_ref[...], block[:width, :], ((1,), (1,)))
        total = term if total is None else total + term
    return total


def grid_rows(blocks, dtype):
    count = len(blocks)

    def kernel(*refs):
        parts = []
        for (_, which), ref in zip(blocks, refs):
            parts += [ref] if which is None else [ref.at[j] for j in which]
        refs[-2][...] = grid_total(parts, refs[-1]).astype(dtype)

    return pl.pallas_call(
        kernel,
        in_specs=[VMEM_SPEC] * count,
        out_specs=VMEM_SPEC,
        out_shape=pltpu.VMEM((CELLS, blocks[0][0].shape[-2] - META), dtype),
        scratch_shapes=WEIGHTS,
        compiler_params=PARAMS,
        name="grid_rows",
    )(*[on_chip(x) for x, _ in blocks])


def grid_pieces(place, blocks, before=None):
    cells = CELLS // 4
    count = len(blocks)
    width = blocks[0][0].shape[-2] - META
    operands = [x for x, _ in blocks] + ([] if before is None else [before])

    def kernel(place_ref, *refs):
        piece_refs, total_ref, weights_ref = refs[-6:-2], refs[-2], refs[-1]
        parts = []
        for (_, which), ref in zip(blocks, refs):
            parts += [ref] if which is None else [ref.at[j] for j in which]
        total_ref[...] = grid_total(parts, weights_ref, None if before is None else refs[count][...])
        for d, piece_ref in enumerate(piece_refs):
            at = pl.ds(pl.multiple_of((place_ref[0] ^ d) * cells, cells), cells)
            piece_ref[...] = total_ref[at, :].astype(jnp.bfloat16)

    return pl.pallas_call(
        kernel,
        in_specs=[SMEM_SPEC] + [VMEM_SPEC] * len(operands),
        out_specs=[VMEM_SPEC] * 4,
        out_shape=[pltpu.VMEM((cells, width), jnp.bfloat16)] * 4,
        scratch_shapes=[pltpu.VMEM((CELLS, width), jnp.float32)] + WEIGHTS,
        compiler_params=PARAMS,
        name="grid_pieces",
    )(place, *[on_chip(x) for x in operands])


def stack(pieces):
    def kernel(*refs):
        for d, ref in enumerate(refs[:-1]):
            refs[-1][d] = ref[...]

    return pl.pallas_call(
        kernel,
        in_specs=[VMEM_SPEC] * len(pieces),
        out_specs=VMEM_SPEC,
        out_shape=pltpu.VMEM((len(pieces), *pieces[0].shape), pieces[0].dtype),
        compiler_params=PARAMS,
        name="stack",
    )(*[on_chip(x) for x in pieces])


def transform_matrix(length, width):
    n = np.arange(length)
    angle = (n[:, None] * n[None, :] % length) * (2.0 * np.pi / length)
    blocks = length // width
    cos = (np.cos(angle) / math.sqrt(length)).reshape(blocks, width, length)
    sin = (np.sin(angle) / math.sqrt(length)).reshape(blocks, width, length)
    whole = np.concatenate([cos, sin], axis=1)
    high = whole.astype(jnp.bfloat16)
    low = (whole - high.astype(np.float64)).astype(jnp.bfloat16)
    return high, low


def transform_kernel(place_ref, x0_ref, x1_ref, x2_ref, x3_ref, late_ref, high_ref, low_ref, out_ref):
    total = None
    for d, ref in enumerate((x0_ref, x1_ref, x2_ref, x3_ref)):
        block = place_ref[0] ^ d
        x = (ref[...].astype(jnp.float32) + late_ref[d].astype(jnp.float32)).astype(jnp.bfloat16)
        width = x.shape[1] // 2
        turned = jnp.concatenate([x[:, width:], -x[:, :width]], axis=1)
        x = jnp.concatenate([x, turned], axis=0)
        for matrix in (high_ref[block], low_ref[block]):
            term = tensor_dot(x, matrix, ((1,), (0,)))
            total = term if total is None else total + term
    cells = out_ref.shape[0]
    out_ref[:, 0, :] = total[:cells]
    out_ref[:, 1, :] = total[cells:]


def transform(place, pieces, late, high, low):
    return pl.pallas_call(
        transform_kernel,
        in_specs=[SMEM_SPEC] + [VMEM_SPEC] * 7,
        out_specs=VMEM_SPEC,
        out_shape=jax.ShapeDtypeStruct((pieces[0].shape[0], 2, high.shape[2]), jnp.float32),
        compiler_params=PARAMS,
        name="transform",
    )(place, *[on_chip(x) for x in (*pieces, late, high, low)])


def on_device_small(visibilities, pair_patch_number, baseline_kernel_taps, kernel_start_cells):
    rows_here, parts_count, channels = visibilities.shape
    patch = pair_patch_number.reshape(rows_here // 128, 128)
    place = lax.axis_index("chan").astype(jnp.int32).reshape(1)
    uv = lax.axis_index("uv").astype(jnp.int32).reshape(1)

    def send(block, pairs, j=0):
        return lax.ppermute(block, "uv", [(2 * a + c, 2 * b + (c ^ j)) for a, b in pairs for c in range(2)])

    def swap(block):
        return lax.ppermute(block, "uv", [(u, u ^ 1) for u in range(8)])

    def exchange(pieces):
        return [pieces[0]] + [lax.ppermute(pieces[d], "chan", [(c, c ^ d) for c in range(4)]) for d in range(1, 4)]

    columns = prepare(patch, baseline_kernel_taps.T, kernel_start_cells.T, visibilities)
    columns2 = swap(columns)
    (first,) = sort_pairs([lambda z: 3 - z], uv, columns, columns2)
    far_in = send(first, [(0, 1), (3, 2)])
    near_in = send(first, [(1, 2), (2, 1)])
    (second,) = sort_pairs([lambda z: at_ends(z, (3 - z) ^ 1, z ^ 1)], uv, columns, columns2, [first])
    second_in = send(second, [(0, 2), (3, 1), (1, 0), (2, 3)])
    last = [lambda z: at_ends(z, z ^ 1, (3 - z) ^ 1), lambda z: z]
    third, own = sort_pairs(last, uv, columns, columns2)
    pair = (0, 1)
    sums = grid_rows([(third, pair)], jnp.float32)
    far_in, sums = lax.optimization_barrier((far_in, sums))
    sums = exchange(grid_pieces(place, [(far_in, pair)], sums))
    onward = [(0, 1), (3, 2), (1, 3), (2, 0)]
    late = send(stack(sums), onward)
    near_in, own, _ = lax.optimization_barrier((near_in, own, sums[0]))
    grid = grid_rows([(own, pair), (near_in, pair)], jnp.float32)
    second_in, grid = lax.optimization_barrier((second_in, grid))
    pieces = exchange(grid_pieces(place, [(second_in, pair)], grid))
    high, low = transform_matrix(4 * channels, channels)
    return transform(place, pieces, late, jnp.asarray(high), jnp.asarray(low))[None]


def kernel_rows(taps_float, offsets_float, cells_side):
    cell_index = jnp.arange(cells_side, dtype=jnp.float32)
    tap_index = jnp.arange(KERNEL_TAPS, dtype=jnp.float32)

    def one_axis(tap_values, opening_pixel):
        matches = (
            cell_index[None, None, :] == opening_pixel[:, None, None] + tap_index[None, :, None]
        ).astype(jnp.float32)
        return jnp.sum(tap_values[:, :, None] * matches, axis=1)

    return (
        one_axis(taps_float[:, :KERNEL_TAPS], offsets_float[:, 0]),
        one_axis(taps_float[:, KERNEL_TAPS : 2 * KERNEL_TAPS], offsets_float[:, 1]),
    )


def angle_table(row_count, col_count, period):
    row_ids = jnp.arange(row_count, dtype=jnp.int32)[:, None]
    col_ids = jnp.arange(col_count, dtype=jnp.int32)[None, :]
    angles = (row_ids * col_ids % period).astype(jnp.float32) * (2.0 * math.pi / period)
    return (jnp.cos(angles), jnp.sin(angles))


def delay_transform(pencil_data):
    leading, cell_count, parts_count, length = pencil_data.shape
    inner_len = 128
    outer_len = length // inner_len
    fine = lax.Precision.HIGH
    wide = jnp.float32
    values = pencil_data.reshape(leading * cell_count, parts_count, outer_len, inner_len)
    real_part = values[:, 0]
    imag_part = values[:, 1]
    cos_outer, sin_outer = angle_table(outer_len, outer_len, outer_len)
    first_real = jnp.einsum(
        "kn,mnj->mkj", cos_outer, real_part, precision=fine, preferred_element_type=wide
    ) + jnp.einsum("kn,mnj->mkj", sin_outer, imag_part, precision=fine, preferred_element_type=wide)
    first_imag = jnp.einsum(
        "kn,mnj->mkj", cos_outer, imag_part, precision=fine, preferred_element_type=wide
    ) - jnp.einsum("kn,mnj->mkj", sin_outer, real_part, precision=fine, preferred_element_type=wide)
    cos_twist, sin_twist = angle_table(outer_len, inner_len, length)
    twisted_real = first_real * cos_twist + first_imag * sin_twist
    twisted_imag = first_imag * cos_twist - first_real * sin_twist
    cos_inner, sin_inner = angle_table(inner_len, inner_len, inner_len)
    final_real = jnp.einsum("mkn,nq->mqk", twisted_real, cos_inner, precision=fine) + jnp.einsum(
        "mkn,nq->mqk", twisted_imag, sin_inner, precision=fine
    )
    final_imag = jnp.einsum("mkn,nq->mqk", twisted_imag, cos_inner, precision=fine) - jnp.einsum(
        "mkn,nq->mqk", twisted_real, sin_inner, precision=fine
    )
    scaling = 1.0 / math.sqrt(length)
    stacked = (
        jnp.stack([final_real.reshape(-1, length), final_imag.reshape(-1, length)], axis=1)
        * scaling
    )
    return stacked.reshape(leading, cell_count, parts_count, length)


def on_device_large(visibilities, pair_patch_number, baseline_kernel_taps, kernel_start_cells):
    rows_here, parts_count, frequency_bins = visibilities.shape
    uv_devices = lax.axis_size("uv")
    capacity = 2 * rows_here // uv_devices
    slot_count = uv_devices * capacity
    flat_layout = visibilities.reshape(rows_here, parts_count * frequency_bins)
    subgrid_list = pair_patch_number[:, 0]
    member = (subgrid_list[:, None] == jnp.arange(uv_devices, dtype=jnp.int32)[None, :]).astype(
        jnp.int32
    )
    preceding = jnp.sum((jnp.cumsum(member, axis=0) - member) * member, axis=1)
    target = subgrid_list * capacity + preceding
    vis_buffer = (
        jnp.zeros((slot_count, parts_count * frequency_bins), jnp.bfloat16)
        .at[target]
        .set(flat_layout)
    )
    vis_buffer = vis_buffer.reshape(uv_devices, capacity, parts_count * frequency_bins)
    u_rows, v_rows = kernel_rows(
        baseline_kernel_taps.astype(jnp.float32),
        kernel_start_cells.astype(jnp.float32),
        SUBGRID_SIDE,
    )
    payload = jnp.concatenate([u_rows, v_rows], axis=1).astype(jnp.bfloat16)
    payload_buffer = jnp.zeros((slot_count, 2 * SUBGRID_SIDE), jnp.bfloat16).at[target].set(payload)
    got_vis, got_payload = (
        lax.all_to_all(vis_buffer, "uv", split_axis=0, concat_axis=0, tiled=True),
        lax.all_to_all(
            payload_buffer.reshape(uv_devices, capacity, 2 * SUBGRID_SIDE),
            "uv",
            split_axis=0,
            concat_axis=0,
            tiled=True,
        ),
    )

    def kernels(payload_block):
        widened = payload_block.astype(jnp.float32)
        return (widened[:, :SUBGRID_SIDE], widened[:, SUBGRID_SIDE:])

    got_vis = got_vis.reshape(slot_count, parts_count * frequency_bins)
    got_payload = got_payload.reshape(slot_count, -1)
    stride = math.gcd(slot_count, 256)
    turn_count = slot_count // stride

    def accumulate(counter, accumulated):
        starting = counter * stride
        vis_block = lax.dynamic_slice_in_dim(got_vis, starting, stride, 0)
        payload_block = lax.dynamic_slice_in_dim(got_payload, starting, stride, 0)
        u_block, v_block = kernels(payload_block)
        weights = (
            (v_block[:, :, None] * u_block[:, None, :])
            .reshape(stride, SUBGRID_SIDE * SUBGRID_SIDE)
            .astype(jnp.bfloat16)
        )
        return accumulated + lax.dot_general(
            weights, vis_block, (((0,), (0,)), ((), ())), preferred_element_type=jnp.float32
        )

    gridded = lax.fori_loop(
        0,
        turn_count,
        accumulate,
        jnp.zeros((SUBGRID_SIDE * SUBGRID_SIDE, parts_count * frequency_bins), jnp.float32),
    )
    gridded = gridded.astype(jnp.bfloat16)
    chan_devices = lax.axis_size("chan")
    pieces = gridded.reshape(
        chan_devices, SUBGRID_SIDE * SUBGRID_SIDE // chan_devices, parts_count, frequency_bins
    )
    return delay_transform(lax.all_to_all(pieces, "chan", split_axis=0, concat_axis=3, tiled=True))


def solution(mesh):
    in_specs = (P("uv", None, "chan"), P("uv", None), P("uv", None), P("uv", None))
    out_specs = P("uv", "chan", None, None)
    small = mesh.shape["uv"] == 8 and mesh.shape["chan"] == 4
    return jax.shard_map(
        on_device_small if small else on_device_large,
        mesh=mesh,
        in_specs=in_specs,
        out_specs=out_specs,
        check_vma=False,
    )
```

```python
import functools
import math

import jax
import jax.numpy as jnp
import numpy as np
from jax import lax
from jax.experimental import pallas as pl
from jax.experimental.pallas import tpu as pltpu
from jax.sharding import PartitionSpec as P

SUBGRID_SIDE = 32
KERNEL_TAPS = 8
CELLS = SUBGRID_SIDE * SUBGRID_SIDE
HALF = 256
SLOTS = 2 * HALF
META = 24
PATCH = 2
RANK = 3
VMEM_LIMIT = 24 << 20
VMEM_SPEC = pl.BlockSpec(memory_space=pltpu.VMEM)
SMEM_SPEC = pl.BlockSpec(memory_space=pltpu.SMEM)
PARAMS = pltpu.CompilerParams(vmem_limit_bytes=VMEM_LIMIT)


def on_chip(x):
    return pltpu.with_memory_space_constraint(x, pltpu.VMEM)


def tensor_dot(a, b, dims):
    return lax.dot_general(a, b, (dims, ((), ())), preferred_element_type=jnp.float32)


def place_rows(patch):
    groups, lanes = patch.shape
    members = jnp.concatenate([(patch == s).astype(jnp.float32) for s in range(8)], axis=0).astype(jnp.bfloat16)
    row = lax.broadcasted_iota(jnp.int32, (lanes, lanes), 0)
    col = lax.broadcasted_iota(jnp.int32, (lanes, lanes), 1)
    before = (row < col).astype(jnp.float32).astype(jnp.bfloat16)
    ahead = tensor_dot(members, before, ((1,), (0,)))
    totals = tensor_dot(members, jnp.ones((lanes, lanes), jnp.bfloat16), ((1,), (0,)))
    r = lax.broadcasted_iota(jnp.int32, (8 * groups, 8 * groups), 0)
    c = lax.broadcasted_iota(jnp.int32, (8 * groups, 8 * groups), 1)
    earlier = ((c < r) & (c // groups == r // groups)).astype(jnp.float32).astype(jnp.bfloat16)
    rank_all = ahead + tensor_dot(earlier, totals.astype(jnp.bfloat16), ((1,), (0,)))
    rank = jnp.zeros((groups, lanes), jnp.float32)
    for s in range(8):
        rank = jnp.where(patch == s, rank_all[s * groups : (s + 1) * groups], rank)
    return rank


def sort_into(target, columns_ref, out_ref):
    lanes = 128
    groups = columns_ref.shape[1] // lanes
    at = columns_ref.shape[0] - META + 2 * KERNEL_TAPS
    data = columns_ref[at : at + META - 2 * KERNEL_TAPS, :].astype(jnp.float32)
    patch = data[PATCH : PATCH + 1, :]
    rank = data[RANK : RANK + 1, :] * HALF + data[RANK + 1 : RANK + 2, :]
    mine = patch == target.astype(jnp.float32)
    slot = lax.broadcasted_iota(jnp.int32, (HALF, lanes), 0).astype(jnp.float32).astype(jnp.bfloat16)
    slot = slot.reshape(HALF // 16, 16, lanes)
    one = jnp.ones((), jnp.bfloat16)
    zero = jnp.zeros((), jnp.bfloat16)

    def selection(h):
        key = jnp.where(mine, rank - h * HALF, -1.0)
        key = jnp.where(key < HALF, key, -1.0)
        pieces = []
        for k in range(groups):
            k16 = jnp.broadcast_to(key[:, k * lanes : (k + 1) * lanes], (16, lanes)).astype(jnp.bfloat16)
            pieces.append(jnp.where(slot == k16[None], one, zero).reshape(HALF, lanes))
        return jnp.concatenate(pieces, axis=1)

    select = jnp.concatenate([selection(0), selection(1)], axis=0)
    out_ref[...] = tensor_dot(columns_ref[...], select, ((1,), (1,))).astype(jnp.bfloat16)


def prepare(patch, taps, starts, vis):
    rows, parts, channels = vis.shape
    width = parts * channels

    def kernel(
        patch_hbm, taps_hbm, starts_hbm, vis_hbm, columns_ref,
        patch_ref, taps_ref, starts_ref, vis_ref, sems,
    ):
        copies = [
            pltpu.make_async_copy(patch_hbm, patch_ref, sems.at[0]),
            pltpu.make_async_copy(vis_hbm, vis_ref, sems.at[1]),
            pltpu.make_async_copy(taps_hbm, taps_ref, sems.at[2]),
            pltpu.make_async_copy(starts_hbm, starts_ref, sems.at[3]),
        ]
        for copy in copies:
            copy.start()
        copies[0].wait()
        patch = patch_ref[...]
        rank = place_rows(patch)
        high = jnp.floor(rank * (1.0 / HALF))
        copies[2].wait()
        copies[3].wait()

        def row_of(x):
            return jnp.concatenate([x[k : k + 1, :] for k in range(x.shape[0])], axis=1)

        columns_ref[width:, :] = jnp.concatenate(
            [
                taps_ref[...].astype(jnp.float32),
                starts_ref[...].astype(jnp.float32),
                row_of(patch.astype(jnp.float32)),
                row_of(high),
                row_of(rank - high * HALF),
                jnp.zeros((META - 2 * KERNEL_TAPS - 5, rows), jnp.float32),
            ],
            axis=0,
        ).astype(jnp.bfloat16)
        copies[1].wait()
        columns_ref[:width, :] = vis_ref[...].reshape(rows, width).T

    in_hbm = [pltpu.with_memory_space_constraint(x, pltpu.HBM) for x in (patch, taps, starts, vis)]
    return pl.pallas_call(
        kernel,
        in_specs=[pl.BlockSpec(memory_space=pl.ANY)] * 4,
        out_specs=VMEM_SPEC,
        out_shape=pltpu.VMEM((width + META, rows), jnp.bfloat16),
        scratch_shapes=[pltpu.VMEM(x.shape, x.dtype) for x in (patch, taps, starts, vis)]
        + [pltpu.SemaphoreType.DMA((4,))],
        compiler_params=PARAMS,
        name="prepare",
    )(*in_hbm)


def at_ends(z, end, middle):
    return jnp.where((z == 0) | (z == 3), end, middle)


def sort_pairs(which, uv, columns, columns2, after=()):
    count = len(which)

    def kernel(uv_ref, columns_ref, columns2_ref, *refs):
        z = uv_ref[0] // 2
        for target_z, ref in zip(which, refs[len(after) :]):
            target = 2 * target_z(z) + uv_ref[0] % 2
            sort_into(target, columns_ref, ref.at[0])
            sort_into(target, columns2_ref, ref.at[1])

    return pl.pallas_call(
        kernel,
        in_specs=[SMEM_SPEC] + [VMEM_SPEC] * (2 + len(after)),
        out_specs=[VMEM_SPEC] * count,
        out_shape=[pltpu.VMEM((2, columns.shape[0], SLOTS), jnp.bfloat16)] * count,
        compiler_params=PARAMS,
        name="sort_pairs",
    )(uv, *[on_chip(x) for x in (columns, columns2, *after)])


def spread(taps, start):
    cell = lax.broadcasted_iota(jnp.int32, (SUBGRID_SIDE, SLOTS), 0).astype(jnp.float32)
    offset = cell - start
    out = jnp.zeros((SUBGRID_SIDE, SLOTS), jnp.float32)
    for i in range(KERNEL_TAPS):
        out = jnp.where(offset == i, taps[i : i + 1, :], out)
    return out


def fill_weights(meta, weights_ref):
    meta = meta.astype(jnp.float32)
    u = spread(meta[:KERNEL_TAPS], meta[2 * KERNEL_TAPS : 2 * KERNEL_TAPS + 1])
    v = spread(meta[KERNEL_TAPS : 2 * KERNEL_TAPS], meta[2 * KERNEL_TAPS + 1 : 2 * KERNEL_TAPS + 2])
    for y in range(SUBGRID_SIDE):
        weights_ref[y * SUBGRID_SIDE : (y + 1) * SUBGRID_SIDE, :] = (v[y : y + 1, :] * u).astype(jnp.bfloat16)


WEIGHTS = [pltpu.VMEM((CELLS, SLOTS), jnp.bfloat16)]


def grid_total(blocks, weights_ref, total=None):
    for block in blocks:
        width = block.shape[0] - META
        fill_weights(block[width:, :], weights_ref)
        term = tensor_dot(weights_ref[...], block[:width, :], ((1,), (1,)))
        total = term if total is None else total + term
    return total


def grid_rows(blocks, dtype):
    count = len(blocks)

    def kernel(*refs):
        parts = []
        for (_, which), ref in zip(blocks, refs):
            parts += [ref] if which is None else [ref.at[j] for j in which]
        refs[-2][...] = grid_total(parts, refs[-1]).astype(dtype)

    return pl.pallas_call(
        kernel,
        in_specs=[VMEM_SPEC] * count,
        out_specs=VMEM_SPEC,
        out_shape=pltpu.VMEM((CELLS, blocks[0][0].shape[-2] - META), dtype),
        scratch_shapes=WEIGHTS,
        compiler_params=PARAMS,
        name="grid_rows",
    )(*[on_chip(x) for x, _ in blocks])


def grid_pieces(place, blocks, before=None):
    cells = CELLS // 4
    count = len(blocks)
    width = blocks[0][0].shape[-2] - META
    operands = [x for x, _ in blocks] + ([] if before is None else [before])

    def kernel(place_ref, *refs):
        piece_refs, total_ref, weights_ref = refs[-6:-2], refs[-2], refs[-1]
        parts = []
        for (_, which), ref in zip(blocks, refs):
            parts += [ref] if which is None else [ref.at[j] for j in which]
        total_ref[...] = grid_total(parts, weights_ref, None if before is None else refs[count][...])
        for d, piece_ref in enumerate(piece_refs):
            at = pl.ds(pl.multiple_of((place_ref[0] ^ d) * cells, cells), cells)
            piece_ref[...] = total_ref[at, :].astype(jnp.bfloat16)

    return pl.pallas_call(
        kernel,
        in_specs=[SMEM_SPEC] + [VMEM_SPEC] * len(operands),
        out_specs=[VMEM_SPEC] * 4,
        out_shape=[pltpu.VMEM((cells, width), jnp.bfloat16)] * 4,
        scratch_shapes=[pltpu.VMEM((CELLS, width), jnp.float32)] + WEIGHTS,
        compiler_params=PARAMS,
        name="grid_pieces",
    )(place, *[on_chip(x) for x in operands])


def stack(pieces):
    def kernel(*refs):
        for d, ref in enumerate(refs[:-1]):
            refs[-1][d] = ref[...]

    return pl.pallas_call(
        kernel,
        in_specs=[VMEM_SPEC] * len(pieces),
        out_specs=VMEM_SPEC,
        out_shape=pltpu.VMEM((len(pieces), *pieces[0].shape), pieces[0].dtype),
        compiler_params=PARAMS,
        name="stack",
    )(*[on_chip(x) for x in pieces])


def transform_matrix(length, width):
    n = np.arange(length)
    angle = (n[:, None] * n[None, :] % length) * (2.0 * np.pi / length)
    blocks = length // width
    cos = (np.cos(angle) / math.sqrt(length)).reshape(blocks, width, length)
    sin = (np.sin(angle) / math.sqrt(length)).reshape(blocks, width, length)
    whole = np.concatenate([cos, sin], axis=1)
    high = whole.astype(jnp.bfloat16)
    low = (whole - high.astype(np.float64)).astype(jnp.bfloat16)
    return high, low


def transform_kernel(place_ref, x0_ref, x1_ref, x2_ref, x3_ref, late_ref, high_ref, low_ref, out_ref):
    total = None
    for d, ref in enumerate((x0_ref, x1_ref, x2_ref, x3_ref)):
        block = place_ref[0] ^ d
        x = (ref[...].astype(jnp.float32) + late_ref[d].astype(jnp.float32)).astype(jnp.bfloat16)
        width = x.shape[1] // 2
        turned = jnp.concatenate([x[:, width:], -x[:, :width]], axis=1)
        x = jnp.concatenate([x, turned], axis=0)
        for matrix in (high_ref[block], low_ref[block]):
            term = tensor_dot(x, matrix, ((1,), (0,)))
            total = term if total is None else total + term
    cells = out_ref.shape[0]
    out_ref[:, 0, :] = total[:cells]
    out_ref[:, 1, :] = total[cells:]


def transform(place, pieces, late, high, low):
    cells, width = pieces[0].shape
    half = cells // 2
    piece = pl.BlockSpec((half, width), lambda i, p: (i, 0))
    matrix = pl.BlockSpec(high.shape, lambda i, p: (0, 0, 0))
    return pl.pallas_call(
        transform_kernel,
        grid_spec=pltpu.PrefetchScalarGridSpec(
            num_scalar_prefetch=1,
            grid=(2,),
            in_specs=[piece] * 4 + [pl.BlockSpec((4, half, width), lambda i, p: (0, i, 0)), matrix, matrix],
            out_specs=pl.BlockSpec((half, 2, high.shape[2]), lambda i, p: (i, 0, 0)),
        ),
        out_shape=jax.ShapeDtypeStruct((cells, 2, high.shape[2]), jnp.float32),
        compiler_params=PARAMS,
        name="transform",
    )(place, *[on_chip(x) for x in (*pieces, late, high, low)])


def on_device_small(visibilities, pair_patch_number, baseline_kernel_taps, kernel_start_cells):
    rows_here, parts_count, channels = visibilities.shape
    patch = pair_patch_number.reshape(rows_here // 128, 128)
    place = lax.axis_index("chan").astype(jnp.int32).reshape(1)
    uv = lax.axis_index("uv").astype(jnp.int32).reshape(1)

    def send(block, pairs, j=0):
        return lax.ppermute(block, "uv", [(2 * a + c, 2 * b + (c ^ j)) for a, b in pairs for c in range(2)])

    def swap(block):
        return lax.ppermute(block, "uv", [(u, u ^ 1) for u in range(8)])

    def exchange(pieces):
        return [pieces[0]] + [lax.ppermute(pieces[d], "chan", [(c, c ^ d) for c in range(4)]) for d in range(1, 4)]

    columns = prepare(patch, baseline_kernel_taps.T, kernel_start_cells.T, visibilities)
    columns2 = swap(columns)
    (first,) = sort_pairs([lambda z: 3 - z], uv, columns, columns2)
    far_in = send(first, [(0, 1), (3, 2)])
    near_in = send(first, [(1, 2), (2, 1)])
    (second,) = sort_pairs([lambda z: at_ends(z, (3 - z) ^ 1, z ^ 1)], uv, columns, columns2, [first])
    second_in = send(second, [(0, 2), (3, 1), (1, 0), (2, 3)])
    last = [lambda z: at_ends(z, z ^ 1, (3 - z) ^ 1), lambda z: z]
    third, own = sort_pairs(last, uv, columns, columns2)
    pair = (0, 1)
    sums = grid_rows([(third, pair)], jnp.float32)
    far_in, sums = lax.optimization_barrier((far_in, sums))
    sums = exchange(grid_pieces(place, [(far_in, pair)], sums))
    onward = [(0, 1), (3, 2), (1, 3), (2, 0)]
    late = send(stack(sums), onward)
    near_in, own, _ = lax.optimization_barrier((near_in, own, sums[0]))
    grid = grid_rows([(own, pair), (near_in, pair)], jnp.float32)
    second_in, grid = lax.optimization_barrier((second_in, grid))
    pieces = exchange(grid_pieces(place, [(second_in, pair)], grid))
    high, low = transform_matrix(4 * channels, channels)
    return transform(place, pieces, late, jnp.asarray(high), jnp.asarray(low))[None]


def kernel_rows(taps_float, offsets_float, cells_side):
    cell_index = jnp.arange(cells_side, dtype=jnp.float32)
    tap_index = jnp.arange(KERNEL_TAPS, dtype=jnp.float32)

    def one_axis(tap_values, opening_pixel):
        matches = (
            cell_index[None, None, :] == opening_pixel[:, None, None] + tap_index[None, :, None]
        ).astype(jnp.float32)
        return jnp.sum(tap_values[:, :, None] * matches, axis=1)

    return (
        one_axis(taps_float[:, :KERNEL_TAPS], offsets_float[:, 0]),
        one_axis(taps_float[:, KERNEL_TAPS : 2 * KERNEL_TAPS], offsets_float[:, 1]),
    )


def angle_table(row_count, col_count, period):
    row_ids = jnp.arange(row_count, dtype=jnp.int32)[:, None]
    col_ids = jnp.arange(col_count, dtype=jnp.int32)[None, :]
    angles = (row_ids * col_ids % period).astype(jnp.float32) * (2.0 * math.pi / period)
    return (jnp.cos(angles), jnp.sin(angles))


def delay_transform(pencil_data):
    leading, cell_count, parts_count, length = pencil_data.shape
    inner_len = 128
    outer_len = length // inner_len
    fine = lax.Precision.HIGH
    wide = jnp.float32
    values = pencil_data.reshape(leading * cell_count, parts_count, outer_len, inner_len)
    real_part = values[:, 0]
    imag_part = values[:, 1]
    cos_outer, sin_outer = angle_table(outer_len, outer_len, outer_len)
    first_real = jnp.einsum(
        "kn,mnj->mkj", cos_outer, real_part, precision=fine, preferred_element_type=wide
    ) + jnp.einsum("kn,mnj->mkj", sin_outer, imag_part, precision=fine, preferred_element_type=wide)
    first_imag = jnp.einsum(
        "kn,mnj->mkj", cos_outer, imag_part, precision=fine, preferred_element_type=wide
    ) - jnp.einsum("kn,mnj->mkj", sin_outer, real_part, precision=fine, preferred_element_type=wide)
    cos_twist, sin_twist = angle_table(outer_len, inner_len, length)
    twisted_real = first_real * cos_twist + first_imag * sin_twist
    twisted_imag = first_imag * cos_twist - first_real * sin_twist
    cos_inner, sin_inner = angle_table(inner_len, inner_len, inner_len)
    final_real = jnp.einsum("mkn,nq->mqk", twisted_real, cos_inner, precision=fine) + jnp.einsum(
        "mkn,nq->mqk", twisted_imag, sin_inner, precision=fine
    )
    final_imag = jnp.einsum("mkn,nq->mqk", twisted_imag, cos_inner, precision=fine) - jnp.einsum(
        "mkn,nq->mqk", twisted_real, sin_inner, precision=fine
    )
    scaling = 1.0 / math.sqrt(length)
    stacked = (
        jnp.stack([final_real.reshape(-1, length), final_imag.reshape(-1, length)], axis=1)
        * scaling
    )
    return stacked.reshape(leading, cell_count, parts_count, length)


def on_device_large(visibilities, pair_patch_number, baseline_kernel_taps, kernel_start_cells):
    rows_here, parts_count, frequency_bins = visibilities.shape
    uv_devices = lax.axis_size("uv")
    capacity = 2 * rows_here // uv_devices
    slot_count = uv_devices * capacity
    flat_layout = visibilities.reshape(rows_here, parts_count * frequency_bins)
    subgrid_list = pair_patch_number[:, 0]
    member = (subgrid_list[:, None] == jnp.arange(uv_devices, dtype=jnp.int32)[None, :]).astype(
        jnp.int32
    )
    preceding = jnp.sum((jnp.cumsum(member, axis=0) - member) * member, axis=1)
    target = subgrid_list * capacity + preceding
    vis_buffer = (
        jnp.zeros((slot_count, parts_count * frequency_bins), jnp.bfloat16)
        .at[target]
        .set(flat_layout)
    )
    vis_buffer = vis_buffer.reshape(uv_devices, capacity, parts_count * frequency_bins)
    u_rows, v_rows = kernel_rows(
        baseline_kernel_taps.astype(jnp.float32),
        kernel_start_cells.astype(jnp.float32),
        SUBGRID_SIDE,
    )
    payload = jnp.concatenate([u_rows, v_rows], axis=1).astype(jnp.bfloat16)
    payload_buffer = jnp.zeros((slot_count, 2 * SUBGRID_SIDE), jnp.bfloat16).at[target].set(payload)
    got_vis, got_payload = (
        lax.all_to_all(vis_buffer, "uv", split_axis=0, concat_axis=0, tiled=True),
        lax.all_to_all(
            payload_buffer.reshape(uv_devices, capacity, 2 * SUBGRID_SIDE),
            "uv",
            split_axis=0,
            concat_axis=0,
            tiled=True,
        ),
    )

    def kernels(payload_block):
        widened = payload_block.astype(jnp.float32)
        return (widened[:, :SUBGRID_SIDE], widened[:, SUBGRID_SIDE:])

    got_vis = got_vis.reshape(slot_count, parts_count * frequency_bins)
    got_payload = got_payload.reshape(slot_count, -1)
    stride = math.gcd(slot_count, 256)
    turn_count = slot_count // stride

    def accumulate(counter, accumulated):
        starting = counter * stride
        vis_block = lax.dynamic_slice_in_dim(got_vis, starting, stride, 0)
        payload_block = lax.dynamic_slice_in_dim(got_payload, starting, stride, 0)
        u_block, v_block = kernels(payload_block)
        weights = (
            (v_block[:, :, None] * u_block[:, None, :])
            .reshape(stride, SUBGRID_SIDE * SUBGRID_SIDE)
            .astype(jnp.bfloat16)
        )
        return accumulated + lax.dot_general(
            weights, vis_block, (((0,), (0,)), ((), ())), preferred_element_type=jnp.float32
        )

    gridded = lax.fori_loop(
        0,
        turn_count,
        accumulate,
        jnp.zeros((SUBGRID_SIDE * SUBGRID_SIDE, parts_count * frequency_bins), jnp.float32),
    )
    gridded = gridded.astype(jnp.bfloat16)
    chan_devices = lax.axis_size("chan")
    pieces = gridded.reshape(
        chan_devices, SUBGRID_SIDE * SUBGRID_SIDE // chan_devices, parts_count, frequency_bins
    )
    return delay_transform(lax.all_to_all(pieces, "chan", split_axis=0, concat_axis=3, tiled=True))


def solution(mesh):
    in_specs = (P("uv", None, "chan"), P("uv", None), P("uv", None), P("uv", None))
    out_specs = P("uv", "chan", None, None)
    small = mesh.shape["uv"] == 8 and mesh.shape["chan"] == 4
    return jax.shard_map(
        on_device_small if small else on_device_large,
        mesh=mesh,
        in_specs=in_specs,
        out_specs=out_specs,
        check_vma=False,
    )
```
